512 devices in a mesh: seq: 32 (over x, y), head: 16 (over z, core).
Axes of the slice: x: 4, y: 8, z: 8, core: 2. Of those that a mesh axis runs over, the one named last changes fastest.
Arguments:
- projected: bfloat16 [3, 4096, 2048], P(None, 'seq', 'head'), may hold values from -6 to 6
- out_grad: bfloat16 [4096, 2048], P('seq', 'head'), may hold values from -6 to 6
- logits: float32 [2, 16, 4096], P(None, 'head', 'seq'), may hold values from -6 to 6
- head_params: float32 [2, 16], P(None, 'head'), may hold values from -12 to 1, as said below
- qkv_weight: bfloat16 [3, 2048, 2048], P(None, None, 'head'), may hold values from -0.1875 to 0.1875
- gate_weight: bfloat16 [2, 16, 2048], P(None, 'head'), may hold values from -1.5 to 1.5
Outputs:
- input_grad: bfloat16 [4096, 2048], P('seq', 'head')
The draws below stay inside these ranges and needn't reach their ends.
Inputs may be any that keep to these rules, and one draw needn't show every extreme that they name: `head_params`: row 0 holds the logarithms of the heads' decay scales, row 1 the decay biases.
All inputs are finite; a program needn't handle non-finite values.
Results may differ from the reference program's by a relative error of at most 0.0034.
Values sent between devices are 32-bit elements; how exact they have to be, the bound alone decides.
A program may use at most 64 MiB of HBM per device.

```python
import math
import jax
import jax.numpy as jnp
from jax import lax

D = 2048
DK = 128
H = 16
BLOCK = 64
TOKENS = 4096


def draw_head_params(key, part):
    rate_key, bias_key = jax.random.split(jax.random.fold_in(key, 17))
    rates = jax.random.uniform(rate_key, (H,), jnp.float32, math.log(0.0001), math.log(0.05))
    biases = jax.random.uniform(bias_key, (H,), jnp.float32, -1.0, 1.0)
    return jnp.stack([rates, biases])


def spiked(values, own_key, source, target, shards_of, factor):
    owner, partner = [(jnp.arange(values.shape[position]) // (values.shape[position] // shards_of)).reshape([-1 if axis == position else 1 for axis in range(values.ndim)]) for position in (source, target)]
    chosen = jax.random.permutation(own_key, shards_of)[partner]
    strong = (owner == chosen) | (owner == (partner + shards_of // 2) % shards_of)
    return jnp.where(strong, factor * values, values)


def level_of(stream_key, dims, cuts, least, top_value):
    factor_of, own = 1.0, jax.random.fold_in(stream_key, 6)
    for dim, parts in cuts:
        heights = jnp.exp(jax.random.uniform(jax.random.fold_in(own, dim), (parts,), jnp.float32, least / len(cuts), top_value / len(cuts)))
        factor_of = factor_of * jnp.repeat(heights, dims[dim] // parts).reshape([-1 if axis == dim else 1 for axis in range(len(dims))])
    return factor_of


def gaussian(key, extent, scale, limit, pieces=(), dtype=jnp.bfloat16):
    entries = jax.random.normal(key, extent, jnp.float32) * scale
    if len(pieces) > 0:
        entries = level_of(key, extent, pieces, -0.22, 0.18) * entries
    return jnp.clip(entries, min=-limit, max=limit).astype(dtype)


def gaussian_with(own_key, shape, width, bound, cuts, heavy, dtype=jnp.bfloat16):
    result = width * jax.random.normal(own_key, shape, jnp.float32)
    if cuts:
        result = result * level_of(own_key, shape, cuts, -0.22, 0.18)
    return jnp.clip(spiked(result, jax.random.fold_in(own_key, 3), *heavy), -bound, bound).astype(dtype)


def setup_inputs(seed: int = 0) -> dict:
    splits = jax.random.split(jax.random.key(seed), 7)
    projected = gaussian(splits[0], (3, TOKENS, H * DK), 1.0, 6.0, ((1, 32), (2, 16)))
    out_grad = gaussian(splits[1], (TOKENS, H * DK), 1.0, 6.0, ((0, 32), (1, 16)))
    logits = gaussian(splits[2], (2, H, TOKENS), 1.5, 6.0, ((1, 16), (2, 32)), jnp.float32)
    head_params = draw_head_params(jax.random.fold_in(splits[6], 71), 0)
    qkv_weight = gaussian_with(splits[4], (3, D, H * DK), D ** -0.5, 0.1875, ((2, 16),), (2, 1, 16, 2.0))
    gate_weight = gaussian(splits[5], (2, H, D), 0.25, 1.5, ((1, 16),))
    return dict(projected=projected, out_grad=out_grad, logits=logits, head_params=head_params, qkv_weight=qkv_weight, gate_weight=gate_weight)


exact_precision = lax.Precision.HIGHEST

def unit_rows(raw_rows):
    return raw_rows * lax.rsqrt(lax.optimization_barrier(jnp.sum(raw_rows * raw_rows, axis=-1, keepdims=True)) + 1.0)

def recurrence(query_raw, key_raw, values, logits, head_params):
    queries = unit_rows(query_raw) * DK ** (-0.5)
    keys = unit_rows(key_raw)
    decay = -jnp.exp(head_params[0])[:, None] * jax.nn.softplus(logits[0] + head_params[1][:, None])
    keep_gate = jnp.exp(decay).T
    write_gate = jax.nn.sigmoid(logits[1]).T
    blocks = TOKENS // BLOCK

    def shape_blocks(array):
        return array.reshape((blocks, BLOCK) + array.shape[1:])
    inputs = tuple((shape_blocks(array) for array in (queries, keys, values, keep_gate, write_gate)))

    def token_step(running_state, token_item):
        single_query_row, single_key_row, value_row, keep_row, write_row = token_item
        retrieved_values = jnp.einsum('xw,xwt->xt', single_key_row, running_state, precision=exact_precision)
        erased = running_state - write_row[:, None, None] * single_key_row[:, :, None] * retrieved_values[:, None, :]
        running_state = keep_row[:, None, None] * erased + write_row[:, None, None] * single_key_row[:, :, None] * value_row[:, None, :]
        return (running_state, jnp.einsum('xw,xwt->xt', single_query_row, running_state, precision=exact_precision))

    @jax.checkpoint
    def block_step(running_state, block_item):
        return lax.scan(token_step, running_state, block_item)
    start_state = jnp.zeros((H, DK, DK), jnp.float32)
    final_state, outputs = lax.scan(block_step, start_state, inputs)
    return outputs.reshape(TOKENS, H, DK)

def reference(projected, out_grad, logits, head_params, qkv_weight, gate_weight):
    raw_inputs = projected.astype(jnp.float32).reshape(3, TOKENS, H, DK)
    out_cotan = out_grad.astype(jnp.float32).reshape(TOKENS, H, DK)

    def forward_fn(query_raw, key_raw, values, logit_rows):
        return recurrence(query_raw, key_raw, values, logit_rows, head_params)
    outputs, pull_back = jax.vjp(forward_fn, raw_inputs[0], raw_inputs[1], raw_inputs[2], logits)
    query_grad, key_grad, value_grad, logit_grad = pull_back(out_cotan)
    stacked_gradient = jnp.stack([query_grad, key_grad, value_grad]).reshape(3, TOKENS, H * DK).astype(jnp.bfloat16)
    total_grad = jnp.zeros((TOKENS, D), jnp.float32)
    for source in range(3):
        total_grad = total_grad + lax.dot_general(stacked_gradient[source], qkv_weight[source], (((1,), (1,)), ((), ())), preferred_element_type=jnp.float32)
    total_grad = total_grad + jnp.einsum('jht,jhd->td', logit_grad, gate_weight.astype(jnp.float32), precision=exact_precision)
    return total_grad.astype(jnp.bfloat16)
```

```python
import functools

import jax
import jax.numpy as jnp
from jax import lax
from jax.experimental import pallas as pl
from jax.experimental.pallas import tpu as pltpu
from jax.sharding import PartitionSpec as P

DK = 128
ROW = 8
f32, bf16 = jnp.float32, jnp.bfloat16
MESH = pl.DeviceIdType.MESH


def split(a):
    high = a.astype(bf16)
    return high, (a - high.astype(f32)).astype(bf16)


def dot(a, b, contract_b):
    return lax.dot_general(
        a, b, (((1,), (contract_b,)), ((), ())), preferred_element_type=f32
    )


def folded(out):
    half = out.shape[1] // 2
    return out[:, :half] + out[:, half:]


def mm(a, b):
    ah, al = split(a)
    bh, bl = split(b)
    right = jnp.concatenate([bh, bl], 1)
    return folded(dot(jnp.concatenate([ah, al], 1), jnp.concatenate([right, right], 0), 0))


def mm_nt(a, b):
    ah, al = split(a)
    bh, bl = split(b)
    right = jnp.concatenate(
        [jnp.concatenate([bh, bh], 1), jnp.concatenate([bl, bl], 1)], 0
    )
    return folded(dot(jnp.concatenate([ah, al], 1), right, 1))


def row_sum(a):
    return jnp.sum(a, axis=1, keepdims=True)


def col_sum(a):
    return jnp.sum(a, axis=0, keepdims=True)


def sigmoid(a):
    return 1.0 / (1.0 + jnp.exp(-a))


def softplus(a):
    return jnp.maximum(a, 0.0) + jnp.log1p(jnp.exp(-jnp.abs(a)))


def indices(n=DK):
    return (
        lax.broadcasted_iota(jnp.int32, (n, n), 0),
        lax.broadcasted_iota(jnp.int32, (n, n), 1),
    )


def inverse_of(lower, row, col):
    eye = jnp.where(row == col, 1.0, 0.0)
    inner = jnp.where((row // 16) == (col // 16), lower, 0.0)
    total = eye - inner
    power = mm(inner, inner)
    total = total + mm(total, power)
    power = mm(power, power)
    total = total + mm(total, power)
    power = mm(power, power)
    total = total + mm(total, power)
    for size in (16, 32):
        cross = jnp.where(
            ((row // (2 * size)) == (col // (2 * size))) & ((row // size) != (col // size)),
            lower,
            0.0,
        )
        total = total - mm(total, mm(cross, total))
    cross = jnp.where((row // 64) != (col // 64), lower, 0.0)
    return total, mm(total, cross)


def kernel(
    nx,
    nz,
    proj_ref,
    do_ref,
    logit_ref,
    hp_ref,
    w_hbm,
    gate_ref,
    out_ref,
    sv,
    cols,
    m_all,
    bf_own,
    bf_all,
    pre,
    suf,
    xf_send,
    xf_recv,
    xb_send,
    xb_recv,
    sg_send,
    sg_all,
    wv,
    own,
    pair_send,
    pair_recv,
    zp_send,
    zp_recv,
    zm_send,
    zm_recv,
    w_sem,
    ag_ss,
    ag_rs,
    a1_ss,
    a1_rs,
    x_ss,
    x_rs,
    a2_ss,
    a2_rs,
    p_ss,
    p_rs,
    zp_ss,
    zp_rs,
    zm_ss,
    zm_rs,
):
    ny, sl = ROW, DK // ROW
    s, h = lax.axis_index("seq"), lax.axis_index("head")
    x, y = s // ny, lax.rem(s, ny)
    z, c = h // 2, lax.rem(h, 2)

    def in_row(d):
        return lax.rem(y + d, ny)

    def row_peer(d):
        return (x * ny + in_row(d), h)

    def x_peer(d):
        return (lax.rem(x + d + nx, nx) * ny + y, h)

    def z_peer(d):
        return (s, lax.rem(z + d + nz, nz) * 2 + c)

    partner = (s, z * 2 + 1 - c)

    def send(src, dst, ss, rs, dev):
        copy = pltpu.make_async_remote_copy(
            src_ref=src, dst_ref=dst, send_sem=ss, recv_sem=rs, device_id=dev, device_id_type=MESH
        )
        copy.start()
        return copy

    w_copy = pltpu.make_async_copy(w_hbm, wv, w_sem)
    w_copy.start()
    barrier = pltpu.get_barrier_semaphore()
    greeted = [row_peer(d) for d in range(1, ny)] + [x_peer(1), x_peer(-1), partner]
    greeted += [z_peer(1), z_peer(-1)]
    for dev in greeted:
        pl.semaphore_signal(barrier, inc=1, device_id=dev, device_id_type=MESH)

    row, col = indices()
    eye = row == col

    def to_col(r):
        return row_sum(jnp.where(eye, r, 0.0))

    def to_row(v):
        return col_sum(jnp.where(eye, v, 0.0))

    hp = hp_ref[...]
    rate = jnp.exp(hp[0:1, 0:1])
    arg = logit_ref[0] + hp[1:2, 0:1]
    decay_row = -rate * softplus(arg)
    beta_row = sigmoid(logit_ref[1])
    beta = to_col(beta_row)
    g = row_sum(jnp.where(col <= row, decay_row, 0.0))
    g_row = to_row(g)
    g_last = g_row[:, DK - 1 : DK]
    lower, upper = row >= col, row <= col
    ratio = jnp.where(lower, jnp.exp(jnp.where(lower, g - g_row, 0.0)), 0.0)
    ratio_t = jnp.where(upper, jnp.exp(jnp.where(upper, g_row - g, 0.0)), 0.0)
    grown = jnp.exp(g)
    rest = jnp.exp(g_last - g)
    last = jnp.exp(g_last)
    k_raw = proj_ref[1].astype(f32)
    k_scale = lax.rsqrt(row_sum(k_raw * k_raw) + 1.0)
    k = k_raw * k_scale
    inner = mm_nt(k, k)
    bare = jnp.where(row > col, ratio * inner, 0.0)
    lo = bare * beta
    half, crossed = inverse_of(lo, row, col)
    y_in = (beta * grown) * k
    half_y = mm(half, y_in)
    w = half_y - mm(crossed, half_y)
    k_end = rest * k
    k_end_t = k_end.T
    m_own = jnp.where(eye, last, 0.0) - mm(k_end_t, w)
    m_all[y] = m_own

    pl.semaphore_wait(barrier, len(greeted))
    ag = [
        send(m_all.at[y], m_all.at[y], ag_ss.at[d], ag_rs.at[d], row_peer(d))
        for d in (4, 3, 5, 2, 6, 1, 7)
    ]

    q_raw = proj_ref[0].astype(f32)
    q_scale = lax.rsqrt(row_sum(q_raw * q_raw) + 1.0)
    qn = q_raw * q_scale
    q = qn * (DK ** (-0.5))
    v = proj_ref[2].astype(f32)
    do = do_ref[...].astype(f32)
    inv = half - mm(crossed, half)
    att = ratio * mm_nt(q, k)
    q_grown = grown * q
    f_off = mm(do.T, q_grown - mm(att, w))
    u = mm(inv, beta * v)
    b_off = mm(u.T, k_end)
    bf_own[:, 0] = b_off.reshape(ny, sl, DK)
    bf_own[:, 1] = f_off.reshape(ny, sl, DK)
    a1 = [
        send(bf_own.at[in_row(d)], bf_all.at[y], a1_ss.at[d], a1_rs.at[d], row_peer(d))
        for d in range(1, ny)
    ]
    bf_all[y] = bf_own[y]
    att_t = ratio_t * mm_nt(k, q)
    saved = (u, w, mm(att_t, do), k_end, inv.T, ratio, ratio_t, bare, lo, att, att_t, k, qn, y_in)
    for n, value in enumerate(saved):
        sv[n] = value
    sv[len(saved)] = jnp.where(row < col, ratio_t * inner * beta_row, 0.0)
    sig = to_col(sigmoid(arg))
    for n, value in enumerate((beta, grown, rest, k_scale, q_scale, sig)):
        cols[n] = jnp.broadcast_to(value, (DK, DK))

    for copy in ag:
        copy.wait_recv()
    for copy in a1:
        copy.wait_recv()

    zeros = jnp.zeros((sl, DK), f32)
    pad = jnp.zeros((DK, DK), f32)
    start = jnp.concatenate([zeros, jnp.where(eye, 1.0, 0.0)], 0)
    fwd = bwd = start
    for n in range(ny):
        j, i = n, ny - 1 - n
        pre[j] = fwd
        suf[i] = bwd
        fwd = mm_nt(fwd, m_all[j]) + jnp.concatenate([bf_all[j, 0], pad], 0)
        bwd = mm(bwd, m_all[i]) + jnp.concatenate([bf_all[i, 1], pad], 0)

    s_row = g_row_in = zeros
    xs = []
    for n in range(nx - 1):
        if n == 0:
            s_out, g_out = fwd[:sl], bwd[:sl]
        else:
            s_out = mm(s_row, fwd[sl:]) + fwd[:sl]
            g_out = mm(g_row_in, bwd[sl:]) + bwd[:sl]
        xf_send[n] = s_out
        xb_send[n] = g_out
        cf = send(xf_send.at[n], xf_recv.at[n], x_ss.at[0, n], x_rs.at[0, n], x_peer(1))
        cb = send(xb_send.at[n], xb_recv.at[n], x_ss.at[1, n], x_rs.at[1, n], x_peer(-1))
        xs += [cf, cb]
        cf.wait_recv()
        cb.wait_recv()
        s_row = jnp.where(x > 0, xf_recv[n], 0.0)
        g_row_in = jnp.where(x < nx - 1, xb_recv[n], 0.0)

    for j in range(ny):
        sg_send[j, 0] = mm(s_row, pre[j, sl:]) + pre[j, :sl]
        sg_send[j, 1] = mm(g_row_in, suf[j, sl:]) + suf[j, :sl]
    a2 = [
        send(sg_send.at[in_row(d)], sg_all.at[y], a2_ss.at[d], a2_rs.at[d], row_peer(d))
        for d in (4, 3, 5, 2, 6, 1, 7)
    ]
    sg_all[y] = sg_send[y]
    for copy in a2:
        copy.wait_recv()
    st = sg_all[:, 0].reshape(DK, DK)
    gt = sg_all[:, 1].reshape(DK, DK)

    u, w, att_do, k_end, inv_t, ratio, ratio_t = (sv[n] for n in range(7))
    fresh = u - mm_nt(w, st)
    d_fresh = att_do + mm_nt(k_end, gt)
    do = do_ref[...].astype(f32)
    d_qg = mm(do, st)
    dx = mm(inv_t, d_fresh)
    d_ke = mm(fresh, gt)
    d_att = jnp.where(lower, mm_nt(do, fresh), 0.0)
    d_att_t = jnp.where(upper, mm_nt(fresh, do), 0.0)
    dy = -mm(dx, st)
    d_lo = jnp.where(row > col, -mm_nt(dx, fresh), 0.0)
    d_lo_t = jnp.where(row < col, -mm_nt(fresh, dx), 0.0)
    bare, lo, att, att_t, k, qn, y_in, lo_t = (sv[n] for n in range(7, 15))
    beta, grown, rest, k_scale, q_scale, sig = (cols[n] for n in range(6))
    q = qn * (DK ** (-0.5))
    v = proj_ref[2].astype(f32)
    sym = d_lo * ratio * beta + d_lo_t * ratio_t * beta_row
    dq = mm(d_att * ratio, k) + grown * d_qg
    dk = mm(d_att_t * ratio_t, q) + mm(sym, k) + (beta * grown) * dy + rest * d_ke
    ke_part = d_ke * k_end
    d_beta = row_sum(d_lo * bare + dx * v + grown * dy * k)
    mixed = d_lo * lo - d_lo_t * lo_t + d_att * att - d_att_t * att_t
    mixed = mixed + dy * y_in + d_qg * (grown * q) - ke_part
    dg_row = to_row(row_sum(mixed))
    tail = col_sum(row_sum(ke_part + last * (st * gt)))
    d_decay = row_sum(jnp.where(col >= row, dg_row, 0.0)) + tail
    d_l0 = -rate * sig * d_decay
    d_l1 = d_beta * beta * (1.0 - beta)
    dq = (q_scale * (DK ** (-0.5))) * (dq - qn * row_sum(dq * qn))
    dk = k_scale * (dk - k * row_sum(dk * k))
    dqk = jnp.concatenate([dq.astype(bf16), dk.astype(bf16)], 1)
    dv = (beta * dx).astype(bf16)

    w_copy.wait()

    def term(target, core):
        at = pl.multiple_of(target * (2 * DK) + core * DK, DK)
        here = pl.ds(at, DK)
        both = jnp.concatenate([wv[0, here, :], wv[1, here, :]], 1)
        out = dot(dqk, both, 1) + dot(dv, wv[2, here, :], 1)
        out = out + d_l0 * gate_ref[0, :, here].astype(f32)
        return out + d_l1 * gate_ref[1, :, here].astype(f32)

    plus, minus = nz // 2, (nz - 1) // 2
    order = []
    for n in range(plus):
        order.append(plus - n)
        if n < minus:
            order.append(nz - minus + n)
    order.append(0)
    pairs = {}
    for d in order:
        target = lax.rem(z + d, nz)
        pair_send[d] = term(target, 1 - c)
        pairs[d] = send(pair_send.at[d], pair_recv.at[d], p_ss.at[d], p_rs.at[d], partner)
        own[d] = term(target, c)
    zs = []
    last_p = last_m = None
    for n in range(plus):
        d = plus - n
        pairs[d].wait_recv()
        value = own[d] + pair_recv[d]
        if last_p is not None:
            last_p.wait_recv()
            value = value + zp_recv[n - 1]
        zp_send[n] = value
        last_p = send(zp_send.at[n], zp_recv.at[n], zp_ss.at[n], zp_rs.at[n], z_peer(1))
        zs.append(last_p)
        if n < minus:
            d = nz - minus + n
            pairs[d].wait_recv()
            value = own[d] + pair_recv[d]
            if last_m is not None:
                last_m.wait_recv()
                value = value + zm_recv[n - 1]
            zm_send[n] = value
            last_m = send(zm_send.at[n], zm_recv.at[n], zm_ss.at[n], zm_rs.at[n], z_peer(-1))
            zs.append(last_m)
    pairs[0].wait_recv()
    total = own[0] + pair_recv[0]
    if last_m is not None:
        last_m.wait_recv()
        total = total + zm_recv[minus - 1]
    last_p.wait_recv()
    out_ref[...] = (total + zp_recv[plus - 1]).astype(bf16)
    for copy in ag + a1 + xs + a2 + list(pairs.values()) + zs:
        copy.wait_send()


def shards(nx, nz, projected, out_grad, logits, head_params, qkv_weight, gate_weight):
    vm = pl.BlockSpec(memory_space=pltpu.VMEM)
    sl, ny = DK // ROW, ROW
    plus, minus = nz // 2, max((nz - 1) // 2, 1)
    dma = pltpu.SemaphoreType.DMA
    scratch = [
        pltpu.VMEM((15, DK, DK), f32),
        pltpu.VMEM((6, DK, DK), f32),
        pltpu.VMEM((ny, DK, DK), f32),
        pltpu.VMEM((ny, 2, sl, DK), f32),
        pltpu.VMEM((ny, 2, sl, DK), f32),
        pltpu.VMEM((ny, sl + DK, DK), f32),
        pltpu.VMEM((ny, sl + DK, DK), f32),
        pltpu.VMEM((nx - 1, sl, DK), f32),
        pltpu.VMEM((nx - 1, sl, DK), f32),
        pltpu.VMEM((nx - 1, sl, DK), f32),
        pltpu.VMEM((nx - 1, sl, DK), f32),
        pltpu.VMEM((ny, 2, sl, DK), f32),
        pltpu.VMEM((ny, 2, sl, DK), f32),
        pltpu.VMEM(qkv_weight.shape, bf16),
        pltpu.VMEM((nz, DK, DK), f32),
        pltpu.VMEM((nz, DK, DK), f32),
        pltpu.VMEM((nz, DK, DK), f32),
        pltpu.VMEM((plus, DK, DK), f32),
        pltpu.VMEM((plus, DK, DK), f32),
        pltpu.VMEM((minus, DK, DK), f32),
        pltpu.VMEM((minus, DK, DK), f32),
        dma(()),
        dma((ny,)),
        dma((ny,)),
        dma((ny,)),
        dma((ny,)),
        dma((2, nx - 1)),
        dma((2, nx - 1)),
        dma((ny,)),
        dma((ny,)),
        dma((nz,)),
        dma((nz,)),
        dma((plus,)),
        dma((plus,)),
        dma((minus,)),
        dma((minus,)),
    ]
    return pl.pallas_call(
        functools.partial(kernel, nx, nz),
        out_shape=jax.ShapeDtypeStruct((DK, DK), bf16),
        in_specs=[vm, vm, vm, vm, pl.BlockSpec(memory_space=pl.ANY), vm],
        out_specs=vm,
        scratch_shapes=scratch,
        compiler_params=pltpu.CompilerParams(
            collective_id=0, has_side_effects=True, vmem_limit_bytes=48 * 1024 * 1024
        ),
        name="delta_backward",
    )(projected, out_grad, logits, head_params, qkv_weight, gate_weight)


def solution(mesh):
    nx, nz = mesh.shape["seq"] // ROW, mesh.shape["head"] // 2
    in_specs = (
        P(None, "seq", "head"),
        P("seq", "head"),
        P(None, "head", "seq"),
        P(None, "head"),
        P(None, None, "head"),
        P(None, "head", None),
    )
    return jax.shard_map(
        functools.partial(shards, nx, nz),
        mesh=mesh,
        in_specs=in_specs,
        out_specs=P("seq", "head"),
        check_vma=False,
    )
```

```python
import functools

import jax
import jax.numpy as jnp
from jax import lax
from jax.experimental import pallas as pl
from jax.experimental.pallas import tpu as pltpu
from jax.sharding import PartitionSpec as P

DK = 128
ROW = 8
HOLD = 4
f32, bf16 = jnp.float32, jnp.bfloat16
MESH = pl.DeviceIdType.MESH


def split(a):
    high = a.astype(bf16)
    return high, (a - high.astype(f32)).astype(bf16)


def dot(a, b, contract_b):
    return lax.dot_general(
        a, b, (((1,), (contract_b,)), ((), ())), preferred_element_type=f32
    )


def folded(out):
    half = out.shape[1] // 2
    return out[:, :half] + out[:, half:]


def mm(a, b):
    ah, al = split(a)
    bh, bl = split(b)
    right = jnp.concatenate([bh, bl], 1)
    return folded(dot(jnp.concatenate([ah, al], 1), jnp.concatenate([right, right], 0), 0))


def mm_nt(a, b):
    ah, al = split(a)
    bh, bl = split(b)
    right = jnp.concatenate(
        [jnp.concatenate([bh, bh], 1), jnp.concatenate([bl, bl], 1)], 0
    )
    return folded(dot(jnp.concatenate([ah, al], 1), right, 1))


def row_sum(a):
    return jnp.sum(a, axis=1, keepdims=True)


def col_sum(a):
    return jnp.sum(a, axis=0, keepdims=True)


def sigmoid(a):
    return 1.0 / (1.0 + jnp.exp(-a))


def softplus(a):
    return jnp.maximum(a, 0.0) + jnp.log1p(jnp.exp(-jnp.abs(a)))


def indices(n=DK):
    return (
        lax.broadcasted_iota(jnp.int32, (n, n), 0),
        lax.broadcasted_iota(jnp.int32, (n, n), 1),
    )


def inverse_of(lower, row, col):
    eye = jnp.where(row == col, 1.0, 0.0)
    inner = jnp.where((row // 16) == (col // 16), lower, 0.0)
    total = eye - inner
    power = mm(inner, inner)
    total = total + mm(total, power)
    power = mm(power, power)
    total = total + mm(total, power)
    power = mm(power, power)
    total = total + mm(total, power)
    for size in (16, 32):
        cross = jnp.where(
            ((row // (2 * size)) == (col // (2 * size))) & ((row // size) != (col // size)),
            lower,
            0.0,
        )
        total = total - mm(total, mm(cross, total))
    cross = jnp.where((row // 64) != (col // 64), lower, 0.0)
    return total, mm(total, cross)


def kernel(
    nx,
    nz,
    proj_hbm,
    do_hbm,
    logit_hbm,
    hp_hbm,
    w_hbm,
    gate_hbm,
    out_ref,
    proj_ref,
    do_ref,
    logit_ref,
    hp_ref,
    gate_ref,
    wv,
    sv,
    cols,
    m_all,
    bf_own,
    bf_all,
    pre,
    suf,
    xm_all,
    xb_own,
    xb_all,
    sg_send,
    sg_all,
    term,
    pair_recv,
    z_send,
    z_recv,
    in_sem,
    ag_ss,
    ag_rs,
    a1_ss,
    a1_rs,
    xm_ss,
    xm_rs,
    xb_ss,
    xb_rs,
    a2_ss,
    a2_rs,
    p_ss,
    p_rs,
    z_ss,
    z_rs,
):
    ny, sl, step = ROW, DK // HOLD, ROW // HOLD
    s, h = lax.axis_index("seq"), lax.axis_index("head")
    x, y = s // ny, lax.rem(s, ny)
    z, c = h // 2, lax.rem(h, 2)
    base = c * (step // 2)
    off = lax.rem(y - base + ny, step)
    holds = off == 0
    slot = lax.rem(y - base + ny, ny) // step

    def row_peer(d):
        return (x * ny + lax.rem(y + d + ny, ny), h)

    def x_peer(d):
        return (lax.rem(x + d, nx) * ny + y, h)

    def z_peer(d):
        return (s, lax.rem(z + d + nz, nz) * 2 + c)

    partner = (s, z * 2 + 1 - c)

    def remote(src, dst, ss, rs, dev):
        return pltpu.make_async_remote_copy(
            src_ref=src, dst_ref=dst, send_sem=ss, recv_sem=rs, device_id=dev, device_id_type=MESH
        )

    barrier = pltpu.get_barrier_semaphore()
    greeted = [row_peer(d) for d in range(1, ny)] + [x_peer(d) for d in range(1, nx)]
    greeted += [partner] + [z_peer(d) for d in (1, -1, 2, -2)]
    for dev in greeted:
        pl.semaphore_signal(barrier, inc=1, device_id=dev, device_id_type=MESH)
    loads = (
        (logit_hbm, logit_ref),
        (hp_hbm, hp_ref),
        (proj_hbm, proj_ref),
        (do_hbm, do_ref),
        (gate_hbm, gate_ref),
        (w_hbm, wv),
    )
    loads = [pltpu.make_async_copy(a, b, in_sem.at[n]) for n, (a, b) in enumerate(loads)]
    for copy in loads:
        copy.start()

    row, col = indices()
    eye = row == col

    def to_col(r):
        return row_sum(jnp.where(eye, r, 0.0))

    def to_row(v):
        return col_sum(jnp.where(eye, v, 0.0))

    loads[0].wait()
    loads[1].wait()
    hp = hp_ref[...]
    rate = jnp.exp(hp[:, 0:1])
    arg = logit_ref[0] + hp[:, 1:2]
    decay_row = -rate * softplus(arg)
    beta_row = sigmoid(logit_ref[1])
    beta = to_col(beta_row)
    g = row_sum(jnp.where(col <= row, decay_row, 0.0))
    g_row = to_row(g)
    g_last = g_row[:, DK - 1 : DK]
    lower, upper = row >= col, row <= col
    ratio = jnp.where(lower, jnp.exp(jnp.where(lower, g - g_row, 0.0)), 0.0)
    ratio_t = jnp.where(upper, jnp.exp(jnp.where(upper, g_row - g, 0.0)), 0.0)
    grown = jnp.exp(g)
    rest = jnp.exp(g_last - g)
    last = jnp.exp(g_last)
    loads[2].wait()
    k_raw = proj_ref[1].astype(f32)
    k_scale = lax.rsqrt(row_sum(k_raw * k_raw) + 1.0)
    k = k_raw * k_scale
    inner = mm_nt(k, k)
    bare = jnp.where(row > col, ratio * inner, 0.0)
    lo = bare * beta
    half, crossed = inverse_of(lo, row, col)
    y_in = (beta * grown) * k
    half_y = mm(half, y_in)
    w = half_y - mm(crossed, half_y)
    k_end = rest * k
    k_end_t = k_end.T
    m_all[y] = jnp.where(eye, last, 0.0) - mm(k_end_t, w)

    pl.semaphore_wait(barrier, len(greeted))
    order = [(HOLD // 2 + n) % HOLD for n in range(HOLD)]

    def to_holders(do):
        for n in order:
            dev = row_peer(step * n - off)
            if n == 0:
                pl.when(jnp.logical_not(holds))(functools.partial(do, n, dev))
            else:
                do(n, dev)

    def from_row(ref, ss, rs):
        for j in range(ny):

            @pl.when(y != j)
            def _():
                remote(ref.at[j], ref.at[j], ss.at[0], rs.at[j], partner).wait_recv()

    def m_copy(n, dev):
        return remote(m_all.at[y], m_all.at[y], ag_ss.at[n], ag_rs.at[y], dev)

    def bf_copy(n, dev):
        to = lax.rem(slot_of(n), HOLD)
        return remote(bf_own.at[to], bf_all.at[y], a1_ss.at[n], a1_rs.at[y], dev)

    def slot_of(n):
        return lax.rem(y + step * n - off - base + ny, ny) // step

    to_holders(lambda n, dev: m_copy(n, dev).start())
    q_raw = proj_ref[0].astype(f32)
    q_scale = lax.rsqrt(row_sum(q_raw * q_raw) + 1.0)
    qn = q_raw * q_scale
    q = qn * (DK ** (-0.5))
    v = proj_ref[2].astype(f32)
    loads[3].wait()
    do = do_ref[...].astype(f32)
    inv = half - mm(crossed, half)
    att = ratio * mm_nt(q, k)
    q_grown = grown * q
    f_off = mm(do.T, q_grown - mm(att, w))
    u = mm(inv, beta * v)
    b_off = mm(u.T, k_end)
    bf_own[:, 0] = b_off.reshape(HOLD, sl, DK)
    bf_own[:, 1] = f_off.reshape(HOLD, sl, DK)
    to_holders(lambda n, dev: bf_copy(n, dev).start())
    bf_all[y] = bf_own[slot]
    att_t = ratio_t * mm_nt(k, q)
    saved = (u, w, mm(att_t, do), k_end, inv.T, ratio, ratio_t, bare, lo, att, att_t, k, qn, y_in)
    for n, value in enumerate(saved):
        sv[n] = value
    sv[len(saved)] = jnp.where(row < col, ratio_t * inner * beta_row, 0.0)
    sig = to_col(sigmoid(arg))
    for n, value in enumerate((beta, grown, rest, k_scale, q_scale, sig)):
        cols[n] = jnp.broadcast_to(value, (DK, DK))
    middle = range(1, nx - 1)

    def xm_copy(d):
        return remote(xm_all.at[x], xm_all.at[x], xm_ss.at[d - 1], xm_rs.at[x], x_peer(d))

    def xb_copy(d):
        at = (x + d) // nx
        return remote(xb_own.at[at], xb_all.at[x], xb_ss.at[d - 1], xb_rs.at[x], x_peer(d))

    in_middle = jnp.logical_and(x > 0, x < nx - 1)
    back = (4, 3, 5, 2, 6, 1, 7) if ny == 8 else tuple(range(1, ny))

    def sg_copy(d):
        to = lax.rem(y + d, ny)
        return remote(sg_send.at[to], sg_all.at[slot], a2_ss.at[d], a2_rs.at[slot], row_peer(d))

    @pl.when(holds)
    def _():
        from_row(m_all, ag_ss, ag_rs)
        from_row(bf_all, a1_ss, a1_rs)
        zeros = jnp.zeros((sl, DK), f32)
        pad = jnp.zeros((DK, DK), f32)
        fwd = bwd = jnp.concatenate([zeros, jnp.where(eye, 1.0, 0.0)], 0)
        for n in range(ny):
            j, i = n, ny - 1 - n
            pre[j] = fwd
            suf[i] = bwd
            fwd = mm_nt(fwd, m_all[j]) + jnp.concatenate([bf_all[j, 0], pad], 0)
            bwd = mm(bwd, m_all[i]) + jnp.concatenate([bf_all[i, 1], pad], 0)
        xm_all[x] = bwd[sl:]
        xb_own[0] = fwd[:sl]
        xb_own[1] = bwd[:sl]
        for d in (2, 1, 3) if nx == 4 else range(1, nx):
            xb_copy(d).start()

        @pl.when(in_middle)
        def _():
            for d in (2, 1, 3) if nx == 4 else range(1, nx):
                xm_copy(d).start()

        xb_all[x] = zeros
        for n in range(nx):

            @pl.when(x != n)
            def _():
                if n in middle:
                    remote(xm_all.at[n], xm_all.at[n], xm_ss.at[0], xm_rs.at[n], partner).wait_recv()
                remote(xb_all.at[n], xb_all.at[n], xb_ss.at[0], xb_rs.at[n], partner).wait_recv()

        s_row = jnp.where(x > 0, xb_all[0], 0.0)
        g_in = jnp.where(x < nx - 1, xb_all[nx - 1], 0.0)
        for n in middle:
            i = nx - 1 - n
            s_row = jnp.where(x > n, mm_nt(s_row, xm_all[n]) + xb_all[n], s_row)
            g_in = jnp.where(x < i, mm(g_in, xm_all[i]) + xb_all[i], g_in)
        for d in back + (0,):
            j = lax.rem(y + d, ny)
            sg_send[j, 0] = mm(s_row, pre[j, sl:]) + pre[j, :sl]
            sg_send[j, 1] = mm(g_in, suf[j, sl:]) + suf[j, :sl]
            if d:
                sg_copy(d).start()
        sg_all[slot] = sg_send[y]

    for n in range(HOLD):

        @pl.when(jnp.logical_or(slot != n, jnp.logical_not(holds)))
        def _():
            remote(sg_all.at[n], sg_all.at[n], a2_ss.at[0], a2_rs.at[n], partner).wait_recv()

    st = sg_all[:, 0].reshape(DK, DK)
    gt = sg_all[:, 1].reshape(DK, DK)

    u, w, att_do, k_end, inv_t, ratio, ratio_t = (sv[n] for n in range(7))
    fresh = u - mm_nt(w, st)
    d_fresh = att_do + mm_nt(k_end, gt)
    do = do_ref[...].astype(f32)
    d_qg = mm(do, st)
    dx = mm(inv_t, d_fresh)
    d_ke = mm(fresh, gt)
    d_att = jnp.where(lower, mm_nt(do, fresh), 0.0)
    d_att_t = jnp.where(upper, mm_nt(fresh, do), 0.0)
    dy = -mm(dx, st)
    d_lo = jnp.where(row > col, -mm_nt(dx, fresh), 0.0)
    d_lo_t = jnp.where(row < col, -mm_nt(fresh, dx), 0.0)
    bare, lo, att, att_t, k, qn, y_in, lo_t = (sv[n] for n in range(7, 15))
    beta, grown, rest, k_scale, q_scale, sig = (cols[n] for n in range(6))
    q = qn * (DK ** (-0.5))
    v = proj_ref[2].astype(f32)
    sym = d_lo * ratio * beta + d_lo_t * ratio_t * beta_row
    dq = mm(d_att * ratio, k) + grown * d_qg
    dk = mm(d_att_t * ratio_t, q) + mm(sym, k) + (beta * grown) * dy + rest * d_ke
    ke_part = d_ke * k_end
    d_beta = row_sum(d_lo * bare + dx * v + grown * dy * k)
    mixed = d_lo * lo - d_lo_t * lo_t + d_att * att - d_att_t * att_t
    mixed = mixed + dy * y_in + d_qg * (grown * q) - ke_part
    dg_row = to_row(row_sum(mixed))
    tail = col_sum(row_sum(ke_part + last * (st * gt)))
    d_decay = row_sum(jnp.where(col >= row, dg_row, 0.0)) + tail
    d_l0 = -rate * sig * d_decay
    d_l1 = d_beta * beta * (1.0 - beta)
    dq = (q_scale * (DK ** (-0.5))) * (dq - qn * row_sum(dq * qn))
    dk = k_scale * (dk - k * row_sum(dk * k))
    dqk = jnp.concatenate([dq.astype(bf16), dk.astype(bf16)], 1)
    dv = (beta * dx).astype(bf16)

    loads[4].wait()
    loads[5].wait()
    wide_l0 = jnp.concatenate([d_l0, d_l0], 1)
    wide_l1 = jnp.concatenate([d_l1, d_l1], 1)

    def compute(d):
        at = pl.multiple_of(lax.rem(z + d + nz, nz) * (2 * DK), 2 * DK)
        here = pl.ds(at, 2 * DK)
        both = jnp.concatenate([wv[0, here, :], wv[1, here, :]], 1)
        out = dot(dqk, both, 1) + dot(dv, wv[2, here, :], 1)
        gates = gate_ref[:, here].astype(f32)
        out = out + wide_l0 * gates[0:1] + wide_l1 * gates[1:2]
        term[d % nz, 0] = out[:, :DK]
        term[d % nz, 1] = out[:, DK:]
        pair(d).start()

    def pair(d):
        d = d % nz
        return remote(term.at[d, 1 - c], pair_recv.at[d], p_ss.at[d], p_rs.at[d], partner)

    def summed(d):
        pair(d).wait_recv()
        return term[d % nz, c] + pair_recv[d % nz]

    part = DK // 2
    msgs = {
        ("far", 1): (0, pl.ds(0, part), 2),
        ("far", -1): (0, pl.ds(part, part), -2),
        ("mid", 1): (1, pl.ds(0, DK), 1),
        ("mid", -1): (2, pl.ds(0, DK), -1),
        ("two", 1): (3, pl.ds(0, DK), 2),
        ("two", -1): (4, pl.ds(0, DK), -2),
        ("one", 1): (5, pl.ds(0, DK), 1),
        ("one", -1): (6, pl.ds(0, DK), -1),
    }

    def msg(name):
        at, rows, d = msgs[name]
        n = list(msgs).index(name)
        return remote(
            z_send.at[at, rows], z_recv.at[at, rows], z_ss.at[n], z_rs.at[n], z_peer(d)
        )

    for d in (4, 3, -3):
        compute(d)
    compute(1)
    z_send[0] = summed(4)
    msg(("far", 1)).start()
    msg(("far", -1)).start()
    compute(-1)
    for sign in (1, -1):
        z_send[msgs["mid", sign][0]] = summed(3 * sign)
        msg(("mid", sign)).start()
    compute(2)
    compute(-2)
    compute(0)
    for sign in (1, -1):
        z_send[msgs["one", sign][0]] = summed(sign)
        msg(("one", sign)).start()
    two = {sign: summed(2 * sign) for sign in (1, -1)}
    total = summed(0)
    for sign in (1, -1):
        at = msgs["two", sign][0]
        msg(("far", sign)).wait_recv()
        msg(("mid", sign)).wait_recv()
        value = two[sign] + z_recv[msgs["mid", sign][0]]
        rows = msgs["far", sign][1]
        z_send[at] = value
        z_send[at, rows] = z_send[at, rows] + z_recv[0, rows]
        msg(("two", sign)).start()
    for sign in (1, -1):
        msg(("one", sign)).wait_recv()
        total = total + z_recv[msgs["one", sign][0]]
    for sign in (1, -1):
        msg(("two", sign)).wait_recv()
        total = total + z_recv[msgs["two", sign][0]]
    out_ref[...] = total.astype(bf16)

    to_holders(lambda n, dev: m_copy(n, dev).wait_send())
    to_holders(lambda n, dev: bf_copy(n, dev).wait_send())

    @pl.when(holds)
    def _():
        for d in range(1, nx):
            xb_copy(d).wait_send()

        @pl.when(in_middle)
        def _():
            for d in range(1, nx):
                xm_copy(d).wait_send()

        for d in range(1, ny):
            sg_copy(d).wait_send()

    for d in range(nz):
        pair(d).wait_send()
    for name in msgs:
        msg(name).wait_send()


def shards(nx, nz, projected, out_grad, logits, head_params, qkv_weight, gate_weight):
    head_params = head_params.T
    gate_weight = gate_weight.transpose(1, 0, 2).reshape(gate_weight.shape[0], -1)
    sl, ny = DK // HOLD, ROW
    dma = pltpu.SemaphoreType.DMA
    scratch = [
        pltpu.VMEM(projected.shape, bf16),
        pltpu.VMEM(out_grad.shape, bf16),
        pltpu.VMEM(logits.shape, f32),
        pltpu.VMEM(head_params.shape, f32),
        pltpu.VMEM(gate_weight.shape, bf16),
        pltpu.VMEM(qkv_weight.shape, bf16),
        pltpu.VMEM((15, DK, DK), f32),
        pltpu.VMEM((6, DK, DK), f32),
        pltpu.VMEM((ny, DK, DK), f32),
        pltpu.VMEM((HOLD, 2, sl, DK), f32),
        pltpu.VMEM((ny, 2, sl, DK), f32),
        pltpu.VMEM((ny, sl + DK, DK), f32),
        pltpu.VMEM((ny, sl + DK, DK), f32),
        pltpu.VMEM((nx, DK, DK), f32),
        pltpu.VMEM((2, sl, DK), f32),
        pltpu.VMEM((nx, sl, DK), f32),
        pltpu.VMEM((ny, 2, sl, DK), f32),
        pltpu.VMEM((HOLD, 2, sl, DK), f32),
        pltpu.VMEM((nz, 2, DK, DK), f32),
        pltpu.VMEM((nz, DK, DK), f32),
        pltpu.VMEM((7, DK, DK), f32),
        pltpu.VMEM((7, DK, DK), f32),
        dma((6,)),
        dma((HOLD,)),
        dma((ny,)),
        dma((HOLD,)),
        dma((ny,)),
        dma((nx - 1,)),
        dma((nx,)),
        dma((nx - 1,)),
        dma((nx,)),
        dma((ny,)),
        dma((HOLD,)),
        dma((nz,)),
        dma((nz,)),
        dma((8,)),
        dma((8,)),
    ]
    return pl.pallas_call(
        functools.partial(kernel, nx, nz),
        out_shape=jax.ShapeDtypeStruct((DK, DK), bf16),
        in_specs=[pl.BlockSpec(memory_space=pltpu.HBM)] * 6,
        out_specs=pl.BlockSpec(memory_space=pltpu.VMEM),
        scratch_shapes=scratch,
        compiler_params=pltpu.CompilerParams(
            collective_id=0, has_side_effects=True, vmem_limit_bytes=67043328
        ),
        name="delta_backward",
    )(projected, out_grad, logits, head_params, qkv_weight, gate_weight)


def solution(mesh):
    nx, nz = mesh.shape["seq"] // ROW, mesh.shape["head"] // 2
    in_specs = (
        P(None, "seq", "head"),
        P("seq", "head"),
        P(None, "head", "seq"),
        P(None, "head"),
        P(None, None, "head"),
        P(None, "head", None),
    )
    return jax.shard_map(
        functools.partial(shards, nx, nz),
        mesh=mesh,
        in_specs=in_specs,
        out_specs=P("seq", "head"),
        check_vma=False,
    )
```

```python
import functools

import jax
import jax.numpy as jnp
from jax import lax
from jax.experimental import pallas as pl
from jax.experimental.pallas import tpu as pltpu
from jax.sharding import PartitionSpec as P

DK = 128
ROW = 8
HOLD = 4
f32, bf16 = jnp.float32, jnp.bfloat16
MESH = pl.DeviceIdType.MESH


def split(a):
    high = a.astype(bf16)
    return high, (a - high.astype(f32)).astype(bf16)


def dot(a, b, contract_b):
    return lax.dot_general(
        a, b, (((1,), (contract_b,)), ((), ())), preferred_element_type=f32
    )


def folded(out):
    half = out.shape[1] // 2
    return out[:, :half] + out[:, half:]


def mm(a, b):
    ah, al = split(a)
    bh, bl = split(b)
    right = jnp.concatenate([bh, bl], 1)
    return folded(dot(jnp.concatenate([ah, al], 1), jnp.concatenate([right, right], 0), 0))


def mm_nt(a, b):
    ah, al = split(a)
    bh, bl = split(b)
    right = jnp.concatenate(
        [jnp.concatenate([bh, bh], 1), jnp.concatenate([bl, bl], 1)], 0
    )
    return folded(dot(jnp.concatenate([ah, al], 1), right, 1))


def row_sum(a):
    return jnp.sum(a, axis=1, keepdims=True)


def col_sum(a):
    return jnp.sum(a, axis=0, keepdims=True)


def sigmoid(a):
    return 1.0 / (1.0 + jnp.exp(-a))


def softplus(a):
    return jnp.maximum(a, 0.0) + jnp.log1p(jnp.exp(-jnp.abs(a)))


def indices(n=DK):
    return (
        lax.broadcasted_iota(jnp.int32, (n, n), 0),
        lax.broadcasted_iota(jnp.int32, (n, n), 1),
    )


def inverse_of(lower, row, col):
    eye = jnp.where(row == col, 1.0, 0.0)
    inner = jnp.where((row // 16) == (col // 16), lower, 0.0)
    total = eye - inner
    power = mm(inner, inner)
    total = total + mm(total, power)
    power = mm(power, power)
    total = total + mm(total, power)
    power = mm(power, power)
    total = total + mm(total, power)
    for size in (16, 32):
        cross = jnp.where(
            ((row // (2 * size)) == (col // (2 * size))) & ((row // size) != (col // size)),
            lower,
            0.0,
        )
        total = total - mm(total, mm(cross, total))
    cross = jnp.where((row // 64) != (col // 64), lower, 0.0)
    return total, mm(total, cross)


def kernel(
    nx,
    nz,
    proj_hbm,
    do_hbm,
    logit_hbm,
    hp_hbm,
    w_hbm,
    gate_hbm,
    out_ref,
    proj_ref,
    do_ref,
    logit_ref,
    hp_ref,
    gate_ref,
    wv,
    sv,
    cols,
    m_all,
    bf_own,
    bf_all,
    pre,
    suf,
    xm_all,
    xb_own,
    xb_all,
    sg_send,
    sg_all,
    term,
    pair_recv,
    z_send,
    z_recv,
    in_sem,
    ag_ss,
    ag_rs,
    a1_ss,
    a1_rs,
    xm_ss,
    xm_rs,
    xb_ss,
    xb_rs,
    a2_ss,
    a2_rs,
    p_ss,
    p_rs,
    z_ss,
    z_rs,
):
    ny, sl, step = ROW, DK // HOLD, ROW // HOLD
    s, h = lax.axis_index("seq"), lax.axis_index("head")
    x, y = s // ny, lax.rem(s, ny)
    z, c = h // 2, lax.rem(h, 2)
    base = c * (step // 2)
    off = lax.rem(y - base + ny, step)
    holds = off == 0
    slot = lax.rem(y - base + ny, ny) // step

    def row_peer(d):
        return (x * ny + lax.rem(y + d + ny, ny), h)

    def x_peer(d):
        return (lax.rem(x + d, nx) * ny + y, h)

    def z_peer(d):
        return (s, lax.rem(z + d + nz, nz) * 2 + c)

    partner = (s, z * 2 + 1 - c)

    def remote(src, dst, ss, rs, dev):
        return pltpu.make_async_remote_copy(
            src_ref=src, dst_ref=dst, send_sem=ss, recv_sem=rs, device_id=dev, device_id_type=MESH
        )

    barrier = pltpu.get_barrier_semaphore()
    greeted = [row_peer(d) for d in range(1, ny)] + [x_peer(d) for d in range(1, nx)]
    greeted += [partner] + [z_peer(d) for d in (1, -1, 2, -2)]
    for dev in greeted:
        pl.semaphore_signal(barrier, inc=1, device_id=dev, device_id_type=MESH)
    loads = (
        (logit_hbm, logit_ref),
        (hp_hbm, hp_ref),
        (proj_hbm, proj_ref),
        (do_hbm, do_ref),
        (gate_hbm, gate_ref),
        (w_hbm, wv),
    )
    loads = [pltpu.make_async_copy(a, b, in_sem.at[n]) for n, (a, b) in enumerate(loads)]
    for copy in loads:
        copy.start()

    row, col = indices()
    eye = row == col

    def to_col(r):
        return row_sum(jnp.where(eye, r, 0.0))

    def to_row(v):
        return col_sum(jnp.where(eye, v, 0.0))

    loads[0].wait()
    loads[1].wait()
    hp = hp_ref[...]
    rate = jnp.exp(hp[:, 0:1])
    arg = logit_ref[0] + hp[:, 1:2]
    decay_row = -rate * softplus(arg)
    beta_row = sigmoid(logit_ref[1])
    beta = to_col(beta_row)
    g = row_sum(jnp.where(col <= row, decay_row, 0.0))
    g_row = to_row(g)
    g_last = g_row[:, DK - 1 : DK]
    lower, upper = row >= col, row <= col
    ratio = jnp.where(lower, jnp.exp(jnp.where(lower, g - g_row, 0.0)), 0.0)
    ratio_t = jnp.where(upper, jnp.exp(jnp.where(upper, g_row - g, 0.0)), 0.0)
    grown = jnp.exp(g)
    rest = jnp.exp(g_last - g)
    last = jnp.exp(g_last)
    loads[2].wait()
    k_raw = proj_ref[1].astype(f32)
    k_scale = lax.rsqrt(row_sum(k_raw * k_raw) + 1.0)
    k = k_raw * k_scale
    inner = mm_nt(k, k)
    bare = jnp.where(row > col, ratio * inner, 0.0)
    lo = bare * beta
    half, crossed = inverse_of(lo, row, col)
    y_in = (beta * grown) * k
    half_y = mm(half, y_in)
    w = half_y - mm(crossed, half_y)
    k_end = rest * k
    k_end_t = k_end.T
    m_all[y] = jnp.where(eye, last, 0.0) - mm(k_end_t, w)

    pl.semaphore_wait(barrier, len(greeted))
    order = [(HOLD // 2 + n) % HOLD for n in range(HOLD)]

    def to_holders(do):
        for n in order:
            dev = row_peer(step * n - off)
            if n == 0:
                pl.when(jnp.logical_not(holds))(functools.partial(do, n, dev))
            else:
                do(n, dev)

    def from_row(ref, ss, rs):
        for j in range(ny):

            @pl.when(y != j)
            def _():
                remote(ref.at[j], ref.at[j], ss.at[0], rs.at[j], partner).wait_recv()

    def m_copy(n, dev):
        return remote(m_all.at[y], m_all.at[y], ag_ss.at[n], ag_rs.at[y], dev)

    def bf_copy(n, dev):
        to = lax.rem(slot_of(n), HOLD)
        return remote(bf_own.at[to], bf_all.at[y], a1_ss.at[n], a1_rs.at[y], dev)

    def slot_of(n):
        return lax.rem(y + step * n - off - base + ny, ny) // step

    to_holders(lambda n, dev: m_copy(n, dev).start())
    q_raw = proj_ref[0].astype(f32)
    q_scale = lax.rsqrt(row_sum(q_raw * q_raw) + 1.0)
    qn = q_raw * q_scale
    q = qn * (DK ** (-0.5))
    v = proj_ref[2].astype(f32)
    loads[3].wait()
    do = do_ref[...].astype(f32)
    inv = half - mm(crossed, half)
    att = ratio * mm_nt(q, k)
    q_grown = grown * q
    f_off = mm(do.T, q_grown - mm(att, w))
    u = mm(inv, beta * v)
    b_off = mm(u.T, k_end)
    bf_own[:, 0] = b_off.reshape(HOLD, sl, DK)
    bf_own[:, 1] = f_off.reshape(HOLD, sl, DK)
    to_holders(lambda n, dev: bf_copy(n, dev).start())
    bf_all[y] = bf_own[slot]
    att_t = ratio_t * mm_nt(k, q)
    saved = (u, w, mm(att_t, do), k_end, inv.T, ratio, ratio_t, bare, lo, att, att_t, k, qn, y_in)
    for n, value in enumerate(saved):
        sv[n] = value
    sv[len(saved)] = jnp.where(row < col, ratio_t * inner * beta_row, 0.0)
    sig = to_col(sigmoid(arg))
    for n, value in enumerate((beta, grown, rest, k_scale, q_scale, sig)):
        cols[n] = jnp.broadcast_to(value, (DK, DK))
    middle = range(1, nx - 1)

    def xm_copy(d):
        return remote(xm_all.at[x], xm_all.at[x], xm_ss.at[d - 1], xm_rs.at[x], x_peer(d))

    def xb_copy(d):
        at = (x + d) // nx
        return remote(xb_own.at[at], xb_all.at[x], xb_ss.at[d - 1], xb_rs.at[x], x_peer(d))

    in_middle = jnp.logical_and(x > 0, x < nx - 1)
    back = (4, 3, 5, 2, 6, 1, 7) if ny == 8 else tuple(range(1, ny))

    def sg_copy(d):
        to = lax.rem(y + d, ny)
        return remote(sg_send.at[to], sg_all.at[slot], a2_ss.at[d], a2_rs.at[slot], row_peer(d))

    @pl.when(holds)
    def _():
        from_row(m_all, ag_ss, ag_rs)
        fwd = bwd = jnp.where(eye, 1.0, 0.0)
        for n in range(ny):
            j, i = n, ny - 1 - n
            pre[j, sl:] = fwd
            suf[i, sl:] = bwd
            fwd = mm_nt(fwd, m_all[j]) if n else m_all[j].T
            bwd = mm(bwd, m_all[i]) if n else m_all[i]
        xm_all[x] = bwd

        @pl.when(in_middle)
        def _():
            for d in (2, 1, 3) if nx == 4 else range(1, nx):
                xm_copy(d).start()

        from_row(bf_all, a1_ss, a1_rs)
        b_sum, f_sum = bf_all[ny - 1, 0], bf_all[0, 1]
        for n in range(1, ny):
            b_sum = b_sum + mm_nt(bf_all[n - 1, 0], suf[n - 1, sl:])
            f_sum = f_sum + mm_nt(bf_all[n, 1], pre[n, sl:])
        xb_own[0] = b_sum
        xb_own[1] = f_sum
        for d in (2, 1, 3) if nx == 4 else range(1, nx):
            xb_copy(d).start()

        zeros = jnp.zeros((sl, DK), f32)
        fwd = bwd = zeros
        for n in range(ny):
            j, i = n, ny - 1 - n
            pre[j, :sl] = fwd
            suf[i, :sl] = bwd
            if n < ny - 1:
                fwd = (mm_nt(fwd, m_all[j]) if n else 0.0) + bf_all[j, 0]
                bwd = (mm(bwd, m_all[i]) if n else 0.0) + bf_all[i, 1]

        xb_all[x] = zeros
        for n in range(nx):

            @pl.when(x != n)
            def _():
                if n in middle:
                    remote(xm_all.at[n], xm_all.at[n], xm_ss.at[0], xm_rs.at[n], partner).wait_recv()
                remote(xb_all.at[n], xb_all.at[n], xb_ss.at[0], xb_rs.at[n], partner).wait_recv()

        s_row = jnp.where(x > 0, xb_all[0], 0.0)
        g_in = jnp.where(x < nx - 1, xb_all[nx - 1], 0.0)
        for n in middle:
            i = nx - 1 - n
            s_row = jnp.where(x > n, mm_nt(s_row, xm_all[n]) + xb_all[n], s_row)
            g_in = jnp.where(x < i, mm(g_in, xm_all[i]) + xb_all[i], g_in)
        for d in back + (0,):
            j = lax.rem(y + d, ny)
            sg_send[j, 0] = mm(s_row, pre[j, sl:]) + pre[j, :sl]
            sg_send[j, 1] = mm(g_in, suf[j, sl:]) + suf[j, :sl]
            if d:
                sg_copy(d).start()
        sg_all[slot] = sg_send[y]

    for n in range(HOLD):

        @pl.when(jnp.logical_or(slot != n, jnp.logical_not(holds)))
        def _():
            remote(sg_all.at[n], sg_all.at[n], a2_ss.at[0], a2_rs.at[n], partner).wait_recv()

    st = sg_all[:, 0].reshape(DK, DK)
    gt = sg_all[:, 1].reshape(DK, DK)

    u, w, att_do, k_end, inv_t, ratio, ratio_t = (sv[n] for n in range(7))
    fresh = u - mm_nt(w, st)
    d_fresh = att_do + mm_nt(k_end, gt)
    do = do_ref[...].astype(f32)
    d_qg = mm(do, st)
    dx = mm(inv_t, d_fresh)
    d_ke = mm(fresh, gt)
    d_att = jnp.where(lower, mm_nt(do, fresh), 0.0)
    d_att_t = jnp.where(upper, mm_nt(fresh, do), 0.0)
    dy = -mm(dx, st)
    d_lo = jnp.where(row > col, -mm_nt(dx, fresh), 0.0)
    d_lo_t = jnp.where(row < col, -mm_nt(fresh, dx), 0.0)
    bare, lo, att, att_t, k, qn, y_in, lo_t = (sv[n] for n in range(7, 15))
    beta, grown, rest, k_scale, q_scale, sig = (cols[n] for n in range(6))
    q = qn * (DK ** (-0.5))
    v = proj_ref[2].astype(f32)
    sym = d_lo * ratio * beta + d_lo_t * ratio_t * beta_row
    dq = mm(d_att * ratio, k) + grown * d_qg
    dk = mm(d_att_t * ratio_t, q) + mm(sym, k) + (beta * grown) * dy + rest * d_ke
    ke_part = d_ke * k_end
    d_beta = row_sum(d_lo * bare + dx * v + grown * dy * k)
    mixed = d_lo * lo - d_lo_t * lo_t + d_att * att - d_att_t * att_t
    mixed = mixed + dy * y_in + d_qg * (grown * q) - ke_part
    dg_row = to_row(row_sum(mixed))
    tail = col_sum(row_sum(ke_part + last * (st * gt)))
    d_decay = row_sum(jnp.where(col >= row, dg_row, 0.0)) + tail
    d_l0 = -rate * sig * d_decay
    d_l1 = d_beta * beta * (1.0 - beta)
    dq = (q_scale * (DK ** (-0.5))) * (dq - qn * row_sum(dq * qn))
    dk = k_scale * (dk - k * row_sum(dk * k))
    dqk = jnp.concatenate([dq.astype(bf16), dk.astype(bf16)], 1)
    dv = (beta * dx).astype(bf16)

    loads[4].wait()
    loads[5].wait()
    wide_l0 = jnp.concatenate([d_l0, d_l0], 1)
    wide_l1 = jnp.concatenate([d_l1, d_l1], 1)

    def compute(d):
        at = pl.multiple_of(lax.rem(z + d + nz, nz) * (2 * DK), 2 * DK)
        here = pl.ds(at, 2 * DK)
        both = jnp.concatenate([wv[0, here, :], wv[1, here, :]], 1)
        out = dot(dqk, both, 1) + dot(dv, wv[2, here, :], 1)
        gates = gate_ref[:, here].astype(f32)
        out = out + wide_l0 * gates[0:1] + wide_l1 * gates[1:2]
        term[d % nz, 0] = out[:, :DK]
        term[d % nz, 1] = out[:, DK:]
        pair(d).start()

    def pair(d):
        d = d % nz
        return remote(term.at[d, 1 - c], pair_recv.at[d], p_ss.at[d], p_rs.at[d], partner)

    def summed(d):
        pair(d).wait_recv()
        return term[d % nz, c] + pair_recv[d % nz]

    part = DK // 2
    msgs = {
        ("far", 1): (0, pl.ds(0, part), 2),
        ("far", -1): (0, pl.ds(part, part), -2),
        ("mid", 1): (1, pl.ds(0, DK), 1),
        ("mid", -1): (2, pl.ds(0, DK), -1),
        ("two", 1): (3, pl.ds(0, DK), 2),
        ("two", -1): (4, pl.ds(0, DK), -2),
        ("one", 1): (5, pl.ds(0, DK), 1),
        ("one", -1): (6, pl.ds(0, DK), -1),
    }

    def msg(name):
        at, rows, d = msgs[name]
        n = list(msgs).index(name)
        return remote(
            z_send.at[at, rows], z_recv.at[at, rows], z_ss.at[n], z_rs.at[n], z_peer(d)
        )

    for d in (4, 3, -3):
        compute(d)
    compute(1)
    z_send[0] = summed(4)
    msg(("far", 1)).start()
    msg(("far", -1)).start()
    compute(-1)
    for sign in (1, -1):
        z_send[msgs["mid", sign][0]] = summed(3 * sign)
        msg(("mid", sign)).start()
    compute(2)
    compute(-2)
    compute(0)
    for sign in (1, -1):
        z_send[msgs["one", sign][0]] = summed(sign)
        msg(("one", sign)).start()
    two = {sign: summed(2 * sign) for sign in (1, -1)}
    total = summed(0)
    for sign in (1, -1):
        at = msgs["two", sign][0]
        msg(("far", sign)).wait_recv()
        msg(("mid", sign)).wait_recv()
        value = two[sign] + z_recv[msgs["mid", sign][0]]
        rows = msgs["far", sign][1]
        z_send[at] = value
        z_send[at, rows] = z_send[at, rows] + z_recv[0, rows]
        msg(("two", sign)).start()
    for sign in (1, -1):
        msg(("one", sign)).wait_recv()
        total = total + z_recv[msgs["one", sign][0]]
    for sign in (1, -1):
        msg(("two", sign)).wait_recv()
        total = total + z_recv[msgs["two", sign][0]]
    out_ref[...] = total.astype(bf16)

    to_holders(lambda n, dev: m_copy(n, dev).wait_send())
    to_holders(lambda n, dev: bf_copy(n, dev).wait_send())

    @pl.when(holds)
    def _():
        for d in range(1, nx):
            xb_copy(d).wait_send()

        @pl.when(in_middle)
        def _():
            for d in range(1, nx):
                xm_copy(d).wait_send()

        for d in range(1, ny):
            sg_copy(d).wait_send()

    for d in range(nz):
        pair(d).wait_send()
    for name in msgs:
        msg(name).wait_send()


def shards(nx, nz, projected, out_grad, logits, head_params, qkv_weight, gate_weight):
    head_params = head_params.T
    gate_weight = gate_weight.transpose(1, 0, 2).reshape(gate_weight.shape[0], -1)
    sl, ny = DK // HOLD, ROW
    dma = pltpu.SemaphoreType.DMA
    scratch = [
        pltpu.VMEM(projected.shape, bf16),
        pltpu.VMEM(out_grad.shape, bf16),
        pltpu.VMEM(logits.shape, f32),
        pltpu.VMEM(head_params.shape, f32),
        pltpu.VMEM(gate_weight.shape, bf16),
        pltpu.VMEM(qkv_weight.shape, bf16),
        pltpu.VMEM((15, DK, DK), f32),
        pltpu.VMEM((6, DK, DK), f32),
        pltpu.VMEM((ny, DK, DK), f32),
        pltpu.VMEM((HOLD, 2, sl, DK), f32),
        pltpu.VMEM((ny, 2, sl, DK), f32),
        pltpu.VMEM((ny, sl + DK, DK), f32),
        pltpu.VMEM((ny, sl + DK, DK), f32),
        pltpu.VMEM((nx, DK, DK), f32),
        pltpu.VMEM((2, sl, DK), f32),
        pltpu.VMEM((nx, sl, DK), f32),
        pltpu.VMEM((ny, 2, sl, DK), f32),
        pltpu.VMEM((HOLD, 2, sl, DK), f32),
        pltpu.VMEM((nz, 2, DK, DK), f32),
        pltpu.VMEM((nz, DK, DK), f32),
        pltpu.VMEM((7, DK, DK), f32),
        pltpu.VMEM((7, DK, DK), f32),
        dma((6,)),
        dma((HOLD,)),
        dma((ny,)),
        dma((HOLD,)),
        dma((ny,)),
        dma((nx - 1,)),
        dma((nx,)),
        dma((nx - 1,)),
        dma((nx,)),
        dma((ny,)),
        dma((HOLD,)),
        dma((nz,)),
        dma((nz,)),
        dma((12,)),
        dma((12,)),
    ]
    return pl.pallas_call(
        functools.partial(kernel, nx, nz),
        out_shape=pltpu.VMEM((DK, DK), bf16),
        in_specs=[pl.BlockSpec(memory_space=pltpu.HBM)] * 6,
        out_specs=pl.BlockSpec(memory_space=pltpu.VMEM),
        scratch_shapes=scratch,
        compiler_params=pltpu.CompilerParams(
            collective_id=0, has_side_effects=True, vmem_limit_bytes=48000000
        ),
        name="delta_backward",
    )(*(pltpu.with_memory_space_constraint(a, pltpu.HBM) for a in (projected, out_grad, logits, head_params, qkv_weight, gate_weight)))


def solution(mesh):
    nx, nz = mesh.shape["seq"] // ROW, mesh.shape["head"] // 2
    in_specs = (
        P(None, "seq", "head"),
        P("seq", "head"),
        P(None, "head", "seq"),
        P(None, "head"),
        P(None, None, "head"),
        P(None, "head", None),
    )
    return jax.shard_map(
        functools.partial(shards, nx, nz),
        mesh=mesh,
        in_specs=in_specs,
        out_specs=P("seq", "head"),
        check_vma=False,
    )
```

```python
import functools

import jax
import jax.numpy as jnp
from jax import lax
from jax.experimental import pallas as pl
from jax.experimental.pallas import tpu as pltpu
from jax.sharding import PartitionSpec as P

DK = 128
ROW = 8
HOLD = 4
f32, bf16 = jnp.float32, jnp.bfloat16
MESH = pl.DeviceIdType.MESH


def split(a):
    high = a.astype(bf16)
    return high, (a - high.astype(f32)).astype(bf16)


def dot(a, b, contract_b):
    return lax.dot_general(
        a, b, (((1,), (contract_b,)), ((), ())), preferred_element_type=f32
    )


def folded(out):
    half = out.shape[1] // 2
    return out[:, :half] + out[:, half:]


def mm(a, b):
    ah, al = split(a)
    bh, bl = split(b)
    right = jnp.concatenate([bh, bl], 1)
    return folded(dot(jnp.concatenate([ah, al], 1), jnp.concatenate([right, right], 0), 0))


def mm_nt(a, b):
    ah, al = split(a)
    bh, bl = split(b)
    right = jnp.concatenate(
        [jnp.concatenate([bh, bh], 1), jnp.concatenate([bl, bl], 1)], 0
    )
    return folded(dot(jnp.concatenate([ah, al], 1), right, 1))


def row_sum(a):
    return jnp.sum(a, axis=1, keepdims=True)


def col_sum(a):
    return jnp.sum(a, axis=0, keepdims=True)


def sigmoid(a):
    return 1.0 / (1.0 + jnp.exp(-a))


def softplus(a):
    return jnp.maximum(a, 0.0) + jnp.log1p(jnp.exp(-jnp.abs(a)))


def indices(n=DK):
    return (
        lax.broadcasted_iota(jnp.int32, (n, n), 0),
        lax.broadcasted_iota(jnp.int32, (n, n), 1),
    )


def inverse_of(lower, row, col):
    eye = jnp.where(row == col, 1.0, 0.0)
    inner = jnp.where((row // 16) == (col // 16), lower, 0.0)
    total = eye - inner
    power = mm(inner, inner)
    total = total + mm(total, power)
    power = mm(power, power)
    total = total + mm(total, power)
    power = mm(power, power)
    total = total + mm(total, power)
    for size in (16, 32):
        cross = jnp.where(
            ((row // (2 * size)) == (col // (2 * size))) & ((row // size) != (col // size)),
            lower,
            0.0,
        )
        total = total - mm(total, mm(cross, total))
    cross = jnp.where((row // 64) != (col // 64), lower, 0.0)
    return total, mm(total, cross)


def kernel(
    nx,
    nz,
    proj_hbm,
    do_hbm,
    logit_hbm,
    hp_hbm,
    w_hbm,
    gate_hbm,
    out_ref,
    proj_ref,
    do_ref,
    logit_ref,
    hp_ref,
    gate_ref,
    wv,
    sv,
    cols,
    m_all,
    bf_own,
    bf_all,
    pre,
    suf,
    xm_all,
    xb_own,
    xb_all,
    sg_send,
    sg_all,
    term,
    pair_recv,
    z_send,
    z_recv,
    in_sem,
    ag_ss,
    ag_rs,
    a1_ss,
    a1_rs,
    xm_ss,
    xm_rs,
    xb_ss,
    xb_rs,
    a2_ss,
    a2_rs,
    p_ss,
    p_rs,
    z_ss,
    z_rs,
):
    ny, sl, step = ROW, DK // HOLD, ROW // HOLD
    s, h = lax.axis_index("seq"), lax.axis_index("head")
    x, y = s // ny, lax.rem(s, ny)
    z, c = h // 2, lax.rem(h, 2)
    base = c * (step // 2)
    off = lax.rem(y - base + ny, step)
    holds = off == 0
    slot = lax.rem(y - base + ny, ny) // step

    def row_peer(d):
        return (x * ny + lax.rem(y + d + ny, ny), h)

    def x_peer(d):
        return (lax.rem(x + d, nx) * ny + y, h)

    def z_peer(d):
        return (s, lax.rem(z + d + nz, nz) * 2 + c)

    partner = (s, z * 2 + 1 - c)

    def remote(src, dst, ss, rs, dev):
        return pltpu.make_async_remote_copy(
            src_ref=src, dst_ref=dst, send_sem=ss, recv_sem=rs, device_id=dev, device_id_type=MESH
        )

    barrier = pltpu.get_barrier_semaphore()
    greeted = [row_peer(d) for d in range(1, ny)] + [x_peer(d) for d in range(1, nx)]
    greeted += [partner] + [z_peer(d) for d in (1, -1, 2, -2)]
    for dev in greeted:
        pl.semaphore_signal(barrier, inc=1, device_id=dev, device_id_type=MESH)
    loads = (
        (logit_hbm, logit_ref),
        (hp_hbm, hp_ref),
        (proj_hbm, proj_ref),
        (do_hbm, do_ref),
        (gate_hbm, gate_ref),
        (w_hbm, wv),
    )
    loads = [pltpu.make_async_copy(a, b, in_sem.at[n]) for n, (a, b) in enumerate(loads)]
    for copy in loads:
        copy.start()

    row, col = indices()
    eye = row == col

    def to_col(r):
        return row_sum(jnp.where(eye, r, 0.0))

    def to_row(v):
        return col_sum(jnp.where(eye, v, 0.0))

    loads[0].wait()
    loads[1].wait()
    hp = hp_ref[...]
    rate = jnp.exp(hp[:, 0:1])
    arg = logit_ref[0] + hp[:, 1:2]
    decay_row = -rate * softplus(arg)
    beta_row = sigmoid(logit_ref[1])
    beta = to_col(beta_row)
    g = row_sum(jnp.where(col <= row, decay_row, 0.0))
    g_row = to_row(g)
    g_last = g_row[:, DK - 1 : DK]
    lower, upper = row >= col, row <= col
    ratio = jnp.where(lower, jnp.exp(jnp.where(lower, g - g_row, 0.0)), 0.0)
    ratio_t = jnp.where(upper, jnp.exp(jnp.where(upper, g_row - g, 0.0)), 0.0)
    grown = jnp.exp(g)
    rest = jnp.exp(g_last - g)
    last = jnp.exp(g_last)
    loads[2].wait()
    k_raw = proj_ref[1].astype(f32)
    k_scale = lax.rsqrt(row_sum(k_raw * k_raw) + 1.0)
    k = k_raw * k_scale
    inner = mm_nt(k, k)
    bare = jnp.where(row > col, ratio * inner, 0.0)
    lo = bare * beta
    half, crossed = inverse_of(lo, row, col)
    y_in = (beta * grown) * k
    half_y = mm(half, y_in)
    w = half_y - mm(crossed, half_y)
    k_end = rest * k
    k_end_t = k_end.T
    m_all[y] = jnp.where(eye, last, 0.0) - mm(k_end_t, w)

    pl.semaphore_wait(barrier, len(greeted))
    order = [(HOLD // 2 + n) % HOLD for n in range(HOLD)]

    def to_holders(do):
        for n in order:
            dev = row_peer(step * n - off)
            if n == 0:
                pl.when(jnp.logical_not(holds))(functools.partial(do, n, dev))
            else:
                do(n, dev)

    def from_row(ref, ss, rs):
        for j in range(ny):

            @pl.when(y != j)
            def _():
                remote(ref.at[j], ref.at[j], ss.at[0], rs.at[j], partner).wait_recv()

    def m_copy(n, dev):
        return remote(m_all.at[y], m_all.at[y], ag_ss.at[n], ag_rs.at[y], dev)

    def bf_copy(n, dev):
        to = lax.rem(slot_of(n), HOLD)
        return remote(bf_own.at[to], bf_all.at[y], a1_ss.at[n], a1_rs.at[y], dev)

    def slot_of(n):
        return lax.rem(y + step * n - off - base + ny, ny) // step

    to_holders(lambda n, dev: m_copy(n, dev).start())
    q_raw = proj_ref[0].astype(f32)
    q_scale = lax.rsqrt(row_sum(q_raw * q_raw) + 1.0)
    qn = q_raw * q_scale
    q = qn * (DK ** (-0.5))
    v = proj_ref[2].astype(f32)
    loads[3].wait()
    do = do_ref[...].astype(f32)
    inv = half - mm(crossed, half)
    att = ratio * mm_nt(q, k)
    q_grown = grown * q
    f_off = mm(do.T, q_grown - mm(att, w))
    u = mm(inv, beta * v)
    b_off = mm(u.T, k_end)
    bf_own[:, 0] = b_off.reshape(HOLD, sl, DK)
    bf_own[:, 1] = f_off.reshape(HOLD, sl, DK)
    to_holders(lambda n, dev: bf_copy(n, dev).start())
    bf_all[y] = bf_own[slot]
    att_t = ratio_t * mm_nt(k, q)
    inv_t = inv.T
    dx_free, dx_state = mm(inv_t, mm(att_t, do)), mm(inv_t, k_end)
    saved = (u, w, dx_free, k_end, dx_state, ratio, ratio_t, bare, lo, att, att_t, k, qn, y_in)
    for n, value in enumerate(saved):
        sv[n] = value
    sv[len(saved)] = jnp.where(row < col, ratio_t * inner * beta_row, 0.0)
    sig = to_col(sigmoid(arg))
    for n, value in enumerate((beta, grown, rest, k_scale, q_scale, sig)):
        cols[n] = jnp.broadcast_to(value, (DK, DK))
    middle = range(1, nx - 1)

    def xm_copy(d):
        return remote(xm_all.at[x], xm_all.at[x], xm_ss.at[d - 1], xm_rs.at[x], x_peer(d))

    def xb_copy(d):
        at = (x + d) // nx
        return remote(xb_own.at[at], xb_all.at[x], xb_ss.at[d - 1], xb_rs.at[x], x_peer(d))

    in_middle = jnp.logical_and(x > 0, x < nx - 1)
    back = (4, 3, 5, 2, 6, 1, 7) if ny == 8 else tuple(range(1, ny))

    def sg_copy(d):
        to = lax.rem(y + d, ny)
        return remote(sg_send.at[to], sg_all.at[slot], a2_ss.at[d], a2_rs.at[slot], row_peer(d))

    @pl.when(holds)
    def _():
        from_row(m_all, ag_ss, ag_rs)
        fwd = bwd = jnp.where(eye, 1.0, 0.0)
        for n in range(ny):
            j, i = n, ny - 1 - n
            pre[j, sl:] = fwd
            suf[i, sl:] = bwd
            fwd = mm_nt(fwd, m_all[j]) if n else m_all[j].T
            bwd = mm(bwd, m_all[i]) if n else m_all[i]
        xm_all[x] = bwd

        @pl.when(in_middle)
        def _():
            for d in (2, 1, 3) if nx == 4 else range(1, nx):
                xm_copy(d).start()

        from_row(bf_all, a1_ss, a1_rs)
        b_sum, f_sum = bf_all[ny - 1, 0], bf_all[0, 1]
        for n in range(1, ny):
            b_sum = b_sum + mm_nt(bf_all[n - 1, 0], suf[n - 1, sl:])
            f_sum = f_sum + mm_nt(bf_all[n, 1], pre[n, sl:])
        xb_own[0] = b_sum
        xb_own[1] = f_sum
        for d in (2, 1, 3) if nx == 4 else range(1, nx):
            xb_copy(d).start()

        zeros = jnp.zeros((sl, DK), f32)
        fwd = bwd = zeros
        for n in range(ny):
            j, i = n, ny - 1 - n
            pre[j, :sl] = fwd
            suf[i, :sl] = bwd
            if n < ny - 1:
                fwd = (mm_nt(fwd, m_all[j]) if n else 0.0) + bf_all[j, 0]
                bwd = (mm(bwd, m_all[i]) if n else 0.0) + bf_all[i, 1]

        xb_all[x] = zeros
        for n in range(nx):

            @pl.when(x != n)
            def _():
                if n in middle:
                    remote(xm_all.at[n], xm_all.at[n], xm_ss.at[0], xm_rs.at[n], partner).wait_recv()
                remote(xb_all.at[n], xb_all.at[n], xb_ss.at[0], xb_rs.at[n], partner).wait_recv()

        s_row = jnp.where(x > 0, xb_all[0], 0.0)
        g_in = jnp.where(x < nx - 1, xb_all[nx - 1], 0.0)
        for n in middle:
            i = nx - 1 - n
            s_row = jnp.where(x > n, mm_nt(s_row, xm_all[n]) + xb_all[n], s_row)
            g_in = jnp.where(x < i, mm(g_in, xm_all[i]) + xb_all[i], g_in)
        for d in back + (0,):
            j = lax.rem(y + d, ny)
            sg_send[j, 0] = mm(s_row, pre[j, sl:]) + pre[j, :sl]
            sg_send[j, 1] = mm(g_in, suf[j, sl:]) + suf[j, :sl]
            if d:
                sg_copy(d).start()
        sg_all[slot] = sg_send[y]

    for n in range(HOLD):

        @pl.when(jnp.logical_or(slot != n, jnp.logical_not(holds)))
        def _():
            remote(sg_all.at[n], sg_all.at[n], a2_ss.at[0], a2_rs.at[n], partner).wait_recv()

    st = sg_all[:, 0].reshape(DK, DK)
    gt = sg_all[:, 1].reshape(DK, DK)

    u, w, dx_free, k_end, dx_state, ratio, ratio_t = (sv[n] for n in range(7))
    fresh = u - mm_nt(w, st)
    do = do_ref[...].astype(f32)
    d_qg = mm(do, st)
    dx = dx_free + mm_nt(dx_state, gt)
    d_ke = mm(fresh, gt)
    d_att = jnp.where(lower, mm_nt(do, fresh), 0.0)
    d_att_t = jnp.where(upper, mm_nt(fresh, do), 0.0)
    dy = -mm(dx, st)
    d_lo = jnp.where(row > col, -mm_nt(dx, fresh), 0.0)
    d_lo_t = jnp.where(row < col, -mm_nt(fresh, dx), 0.0)
    bare, lo, att, att_t, k, qn, y_in, lo_t = (sv[n] for n in range(7, 15))
    beta, grown, rest, k_scale, q_scale, sig = (cols[n] for n in range(6))
    q = qn * (DK ** (-0.5))
    v = proj_ref[2].astype(f32)
    sym = d_lo * ratio * beta + d_lo_t * ratio_t * beta_row
    dq = mm(d_att * ratio, k) + grown * d_qg
    dk = mm(d_att_t * ratio_t, q) + mm(sym, k) + (beta * grown) * dy + rest * d_ke
    ke_part = d_ke * k_end
    d_beta = row_sum(d_lo * bare + dx * v + grown * dy * k)
    mixed = d_lo * lo - d_lo_t * lo_t + d_att * att - d_att_t * att_t
    mixed = mixed + dy * y_in + d_qg * (grown * q) - ke_part
    dg_row = to_row(row_sum(mixed))
    tail = col_sum(row_sum(ke_part + last * (st * gt)))
    d_decay = row_sum(jnp.where(col >= row, dg_row, 0.0)) + tail
    d_l0 = -rate * sig * d_decay
    d_l1 = d_beta * beta * (1.0 - beta)
    dq = (q_scale * (DK ** (-0.5))) * (dq - qn * row_sum(dq * qn))
    dk = k_scale * (dk - k * row_sum(dk * k))
    dqk = jnp.concatenate([dq.astype(bf16), dk.astype(bf16)], 1)
    dv = (beta * dx).astype(bf16)

    loads[4].wait()
    loads[5].wait()
    wide_l0 = jnp.concatenate([d_l0, d_l0], 1)
    wide_l1 = jnp.concatenate([d_l1, d_l1], 1)

    def compute(d):
        at = pl.multiple_of(lax.rem(z + d + nz, nz) * (2 * DK), 2 * DK)
        here = pl.ds(at, 2 * DK)
        both = jnp.concatenate([wv[0, here, :], wv[1, here, :]], 1)
        out = dot(dqk, both, 1) + dot(dv, wv[2, here, :], 1)
        gates = gate_ref[:, here].astype(f32)
        out = out + wide_l0 * gates[0:1] + wide_l1 * gates[1:2]
        term[d % nz, 0] = out[:, :DK]
        term[d % nz, 1] = out[:, DK:]
        pair(d).start()

    def pair(d):
        d = d % nz
        return remote(term.at[d, 1 - c], pair_recv.at[d], p_ss.at[d], p_rs.at[d], partner)

    def summed(d):
        pair(d).wait_recv()
        return term[d % nz, c] + pair_recv[d % nz]

    part = DK // 2
    msgs = {
        ("far", 1): (0, pl.ds(0, part), 2),
        ("far", -1): (0, pl.ds(part, part), -2),
        ("mid", 1): (1, pl.ds(0, DK), 1),
        ("mid", -1): (2, pl.ds(0, DK), -1),
        ("two", 1): (3, pl.ds(0, DK), 2),
        ("two", -1): (4, pl.ds(0, DK), -2),
        ("one", 1): (5, pl.ds(0, DK), 1),
        ("one", -1): (6, pl.ds(0, DK), -1),
    }

    def msg(name):
        at, rows, d = msgs[name]
        n = list(msgs).index(name)
        return remote(
            z_send.at[at, rows], z_recv.at[at, rows], z_ss.at[n], z_rs.at[n], z_peer(d)
        )

    for d in (4, 3, -3):
        compute(d)
    compute(1)
    z_send[0] = summed(4)
    msg(("far", 1)).start()
    msg(("far", -1)).start()
    compute(-1)
    for sign in (1, -1):
        z_send[msgs["mid", sign][0]] = summed(3 * sign)
        msg(("mid", sign)).start()
    compute(2)
    compute(-2)
    compute(0)
    for sign in (1, -1):
        z_send[msgs["one", sign][0]] = summed(sign)
        msg(("one", sign)).start()
    two = {sign: summed(2 * sign) for sign in (1, -1)}
    total = summed(0)
    for sign in (1, -1):
        at = msgs["two", sign][0]
        msg(("far", sign)).wait_recv()
        msg(("mid", sign)).wait_recv()
        value = two[sign] + z_recv[msgs["mid", sign][0]]
        rows = msgs["far", sign][1]
        z_send[at] = value
        z_send[at, rows] = z_send[at, rows] + z_recv[0, rows]
        msg(("two", sign)).start()
    for sign in (1, -1):
        msg(("one", sign)).wait_recv()
        total = total + z_recv[msgs["one", sign][0]]
    for sign in (1, -1):
        msg(("two", sign)).wait_recv()
        total = total + z_recv[msgs["two", sign][0]]
    out_ref[...] = total.astype(bf16)

    to_holders(lambda n, dev: m_copy(n, dev).wait_send())
    to_holders(lambda n, dev: bf_copy(n, dev).wait_send())

    @pl.when(holds)
    def _():
        for d in range(1, nx):
            xb_copy(d).wait_send()

        @pl.when(in_middle)
        def _():
            for d in range(1, nx):
                xm_copy(d).wait_send()

        for d in range(1, ny):
            sg_copy(d).wait_send()

    for d in range(nz):
        pair(d).wait_send()
    for name in msgs:
        msg(name).wait_send()


def shards(nx, nz, projected, out_grad, logits, head_params, qkv_weight, gate_weight):
    head_params = head_params.T
    gate_weight = gate_weight.transpose(1, 0, 2).reshape(gate_weight.shape[0], -1)
    sl, ny = DK // HOLD, ROW
    dma = pltpu.SemaphoreType.DMA
    scratch = [
        pltpu.VMEM(projected.shape, bf16),
        pltpu.VMEM(out_grad.shape, bf16),
        pltpu.VMEM(logits.shape, f32),
        pltpu.VMEM(head_params.shape, f32),
        pltpu.VMEM(gate_weight.shape, bf16),
        pltpu.VMEM(qkv_weight.shape, bf16),
        pltpu.VMEM((15, DK, DK), f32),
        pltpu.VMEM((6, DK, DK), f32),
        pltpu.VMEM((ny, DK, DK), f32),
        pltpu.VMEM((HOLD, 2, sl, DK), f32),
        pltpu.VMEM((ny, 2, sl, DK), f32),
        pltpu.VMEM((ny, sl + DK, DK), f32),
        pltpu.VMEM((ny, sl + DK, DK), f32),
        pltpu.VMEM((nx, DK, DK), f32),
        pltpu.VMEM((2, sl, DK), f32),
        pltpu.VMEM((nx, sl, DK), f32),
        pltpu.VMEM((ny, 2, sl, DK), f32),
        pltpu.VMEM((HOLD, 2, sl, DK), f32),
        pltpu.VMEM((nz, 2, DK, DK), f32),
        pltpu.VMEM((nz, DK, DK), f32),
        pltpu.VMEM((7, DK, DK), f32),
        pltpu.VMEM((7, DK, DK), f32),
        dma((6,)),
        dma((HOLD,)),
        dma((ny,)),
        dma((HOLD,)),
        dma((ny,)),
        dma((nx - 1,)),
        dma((nx,)),
        dma((nx - 1,)),
        dma((nx,)),
        dma((ny,)),
        dma((HOLD,)),
        dma((nz,)),
        dma((nz,)),
        dma((12,)),
        dma((12,)),
    ]
    return pl.pallas_call(
        functools.partial(kernel, nx, nz),
        out_shape=pltpu.VMEM((DK, DK), bf16),
        in_specs=[pl.BlockSpec(memory_space=pltpu.HBM)] * 6,
        out_specs=pl.BlockSpec(memory_space=pltpu.VMEM),
        scratch_shapes=scratch,
        compiler_params=pltpu.CompilerParams(
            collective_id=0, has_side_effects=True, vmem_limit_bytes=48000000
        ),
        name="delta_backward",
    )(*(pltpu.with_memory_space_constraint(a, pltpu.HBM) for a in (projected, out_grad, logits, head_params, qkv_weight, gate_weight)))


def solution(mesh):
    nx, nz = mesh.shape["seq"] // ROW, mesh.shape["head"] // 2
    in_specs = (
        P(None, "seq", "head"),
        P("seq", "head"),
        P(None, "head", "seq"),
        P(None, "head"),
        P(None, None, "head"),
        P(None, "head", None),
    )
    return jax.shard_map(
        functools.partial(shards, nx, nz),
        mesh=mesh,
        in_specs=in_specs,
        out_specs=P("seq", "head"),
        check_vma=False,
    )
```

```python
import functools

import jax
import jax.numpy as jnp
from jax import lax
from jax.experimental import pallas as pl
from jax.experimental.pallas import tpu as pltpu
from jax.sharding import PartitionSpec as P

DK = 128
ROW = 8
HOLD = 4
f32, bf16 = jnp.float32, jnp.bfloat16
MESH = pl.DeviceIdType.MESH


def split(a):
    high = a.astype(bf16)
    return high, (a - high.astype(f32)).astype(bf16)


def dot(a, b, contract_b):
    return lax.dot_general(
        a, b, (((1,), (contract_b,)), ((), ())), preferred_element_type=f32
    )


def folded(out):
    half = out.shape[1] // 2
    return out[:, :half] + out[:, half:]


def mm(a, b):
    ah, al = split(a)
    bh, bl = split(b)
    right = jnp.concatenate([bh, bl], 1)
    return folded(dot(jnp.concatenate([ah, al], 1), jnp.concatenate([right, right], 0), 0))


def mm_nt(a, b):
    ah, al = split(a)
    bh, bl = split(b)
    right = jnp.concatenate(
        [jnp.concatenate([bh, bh], 1), jnp.concatenate([bl, bl], 1)], 0
    )
    return folded(dot(jnp.concatenate([ah, al], 1), right, 1))


def row_sum(a):
    return jnp.sum(a, axis=1, keepdims=True)


def col_sum(a):
    return jnp.sum(a, axis=0, keepdims=True)


def sigmoid(a):
    return 1.0 / (1.0 + jnp.exp(-a))


def softplus(a):
    return jnp.maximum(a, 0.0) + jnp.log1p(jnp.exp(-jnp.abs(a)))


def indices(n=DK):
    return (
        lax.broadcasted_iota(jnp.int32, (n, n), 0),
        lax.broadcasted_iota(jnp.int32, (n, n), 1),
    )


def inverse_of(lower, row, col):
    eye = jnp.where(row == col, 1.0, 0.0)
    inner = jnp.where((row // 16) == (col // 16), lower, 0.0)
    total = eye - inner
    power = mm(inner, inner)
    total = total + mm(total, power)
    power = mm(power, power)
    total = total + mm(total, power)
    power = mm(power, power)
    total = total + mm(total, power)
    for size in (16, 32):
        cross = jnp.where(
            ((row // (2 * size)) == (col // (2 * size))) & ((row // size) != (col // size)),
            lower,
            0.0,
        )
        total = total - mm(total, mm(cross, total))
    cross = jnp.where((row // 64) != (col // 64), lower, 0.0)
    return total, mm(total, cross)


def kernel(
    nx,
    nz,
    proj_hbm,
    do_hbm,
    logit_hbm,
    hp_hbm,
    w_hbm,
    gate_hbm,
    out_ref,
    proj_ref,
    do_ref,
    logit_ref,
    hp_ref,
    gate_ref,
    wv,
    sv,
    cols,
    m_all,
    bf_own,
    bf_all,
    pre,
    suf,
    xm_all,
    xb_own,
    xb_all,
    sg_send,
    sg_all,
    term,
    pair_recv,
    z_send,
    z_recv,
    in_sem,
    ag_ss,
    ag_rs,
    a1_ss,
    a1_rs,
    xm_ss,
    xm_rs,
    xb_ss,
    xb_rs,
    a2_ss,
    a2_rs,
    p_ss,
    p_rs,
    z_ss,
    z_rs,
):
    ny, sl, step = ROW, DK // HOLD, ROW // HOLD
    s, h = lax.axis_index("seq"), lax.axis_index("head")
    x, y = s // ny, lax.rem(s, ny)
    z, c = h // 2, lax.rem(h, 2)
    base = c * (step // 2)
    off = lax.rem(y - base + ny, step)
    holds = off == 0
    slot = lax.rem(y - base + ny, ny) // step

    def row_peer(d):
        return (x * ny + lax.rem(y + d + ny, ny), h)

    def x_peer(d):
        return (lax.rem(x + d, nx) * ny + y, h)

    def z_peer(d):
        return (s, lax.rem(z + d + nz, nz) * 2 + c)

    partner = (s, z * 2 + 1 - c)

    def remote(src, dst, ss, rs, dev):
        return pltpu.make_async_remote_copy(
            src_ref=src, dst_ref=dst, send_sem=ss, recv_sem=rs, device_id=dev, device_id_type=MESH
        )

    barrier = pltpu.get_barrier_semaphore()
    greeted = [row_peer(d) for d in range(1, ny)] + [x_peer(d) for d in range(1, nx)]
    greeted += [partner] + [z_peer(d) for d in (1, -1, 2, -2)]
    for dev in greeted:
        pl.semaphore_signal(barrier, inc=1, device_id=dev, device_id_type=MESH)
    loads = (
        (logit_hbm, logit_ref),
        (hp_hbm, hp_ref),
        (proj_hbm, proj_ref),
        (do_hbm, do_ref),
        (gate_hbm, gate_ref),
        (w_hbm, wv),
    )
    loads = [pltpu.make_async_copy(a, b, in_sem.at[n]) for n, (a, b) in enumerate(loads)]
    for copy in loads:
        copy.start()

    row, col = indices()
    eye = row == col

    def to_col(r):
        return row_sum(jnp.where(eye, r, 0.0))

    def to_row(v):
        return col_sum(jnp.where(eye, v, 0.0))

    loads[0].wait()
    loads[1].wait()
    hp = hp_ref[...]
    rate = jnp.exp(hp[:, 0:1])
    arg = logit_ref[0] + hp[:, 1:2]
    decay_row = -rate * softplus(arg)
    beta_row = sigmoid(logit_ref[1])
    beta = to_col(beta_row)
    g = row_sum(jnp.where(col <= row, decay_row, 0.0))
    g_row = to_row(g)
    g_last = g_row[:, DK - 1 : DK]
    lower, upper = row >= col, row <= col
    ratio = jnp.where(lower, jnp.exp(jnp.where(lower, g - g_row, 0.0)), 0.0)
    ratio_t = jnp.where(upper, jnp.exp(jnp.where(upper, g_row - g, 0.0)), 0.0)
    grown = jnp.exp(g)
    rest = jnp.exp(g_last - g)
    last = jnp.exp(g_last)
    loads[2].wait()
    k_raw = proj_ref[1].astype(f32)
    k_scale = lax.rsqrt(row_sum(k_raw * k_raw) + 1.0)
    k = k_raw * k_scale
    inner = mm_nt(k, k)
    bare = jnp.where(row > col, ratio * inner, 0.0)
    lo = bare * beta
    half, crossed = inverse_of(lo, row, col)
    y_in = (beta * grown) * k
    half_y = mm(half, y_in)
    w = half_y - mm(crossed, half_y)
    k_end = rest * k
    k_end_t = k_end.T
    m_all[y] = jnp.where(eye, last, 0.0) - mm(k_end_t, w)

    pl.semaphore_wait(barrier, len(greeted))
    order = [(HOLD // 2 + n) % HOLD for n in range(HOLD)]

    def to_holders(do):
        for n in order:
            dev = row_peer(step * n - off)
            if n == 0:
                pl.when(jnp.logical_not(holds))(functools.partial(do, n, dev))
            else:
                do(n, dev)

    def from_row(ref, ss, rs):
        for j in range(ny):

            @pl.when(y != j)
            def _():
                remote(ref.at[j], ref.at[j], ss.at[0], rs.at[j], partner).wait_recv()

    def m_copy(n, dev):
        return remote(m_all.at[y], m_all.at[y], ag_ss.at[n], ag_rs.at[y], dev)

    def bf_copy(n, dev):
        to = lax.rem(slot_of(n), HOLD)
        return remote(bf_own.at[to], bf_all.at[y], a1_ss.at[n], a1_rs.at[y], dev)

    def slot_of(n):
        return lax.rem(y + step * n - off - base + ny, ny) // step

    to_holders(lambda n, dev: m_copy(n, dev).start())
    q_raw = proj_ref[0].astype(f32)
    q_scale = lax.rsqrt(row_sum(q_raw * q_raw) + 1.0)
    qn = q_raw * q_scale
    q = qn * (DK ** (-0.5))
    v = proj_ref[2].astype(f32)
    loads[3].wait()
    do = do_ref[...].astype(f32)
    inv = half - mm(crossed, half)
    att = ratio * mm_nt(q, k)
    q_grown = grown * q
    f_off = mm(do.T, q_grown - mm(att, w))
    u = mm(inv, beta * v)
    b_off = mm(u.T, k_end)
    bf_own[:, 0] = b_off.reshape(HOLD, sl, DK)
    bf_own[:, 1] = f_off.reshape(HOLD, sl, DK)
    to_holders(lambda n, dev: bf_copy(n, dev).start())
    bf_all[y] = bf_own[slot]
    att_t = ratio_t * mm_nt(k, q)
    inv_t = inv.T
    dx_free, dx_state = mm(inv_t, mm(att_t, do)), mm(inv_t, k_end)
    saved = (u, w, dx_free, k_end, dx_state, ratio, ratio_t, bare, lo, att, att_t, k, qn, y_in)
    for n, value in enumerate(saved):
        sv[n] = value
    sv[len(saved)] = jnp.where(row < col, ratio_t * inner * beta_row, 0.0)
    sig = to_col(sigmoid(arg))
    for n, value in enumerate((beta, grown, rest, k_scale, q_scale, sig)):
        cols[n] = jnp.broadcast_to(value, (DK, DK))
    middle = range(1, nx - 1)

    def xm_copy(d):
        return remote(xm_all.at[x], xm_all.at[x], xm_ss.at[d - 1], xm_rs.at[x], x_peer(d))

    def xb_copy(d):
        at = (x + d) // nx
        return remote(xb_own.at[at], xb_all.at[x], xb_ss.at[d - 1], xb_rs.at[x], x_peer(d))

    in_middle = jnp.logical_and(x > 0, x < nx - 1)
    back = (4, 3, 5, 2, 6, 1, 7) if ny == 8 else tuple(range(1, ny))

    def sg_copy(d):
        to = lax.rem(y + d, ny)
        return remote(sg_send.at[to], sg_all.at[slot], a2_ss.at[d], a2_rs.at[slot], row_peer(d))

    @pl.when(holds)
    def _():
        from_row(m_all, ag_ss, ag_rs)
        fwd = bwd = jnp.where(eye, 1.0, 0.0)
        for n in range(ny):
            j, i = n, ny - 1 - n
            pre[j, sl:] = fwd
            suf[i, sl:] = bwd
            fwd = mm_nt(fwd, m_all[j]) if n else m_all[j].T
            bwd = mm(bwd, m_all[i]) if n else m_all[i]
        xm_all[x] = bwd

        @pl.when(in_middle)
        def _():
            for d in (2, 1, 3) if nx == 4 else range(1, nx):
                xm_copy(d).start()

        from_row(bf_all, a1_ss, a1_rs)
        b_sum, f_sum = bf_all[ny - 1, 0], bf_all[0, 1]
        for n in range(1, ny):
            b_sum = b_sum + mm_nt(bf_all[n - 1, 0], suf[n - 1, sl:])
            f_sum = f_sum + mm_nt(bf_all[n, 1], pre[n, sl:])
        xb_own[0] = b_sum
        xb_own[1] = f_sum
        for d in (2, 1, 3) if nx == 4 else range(1, nx):
            xb_copy(d).start()

        zeros = jnp.zeros((sl, DK), f32)
        fwd = bwd = zeros
        for n in range(ny):
            j, i = n, ny - 1 - n
            pre[j, :sl] = fwd
            suf[i, :sl] = bwd
            if n < ny - 1:
                fwd = (mm_nt(fwd, m_all[j]) if n else 0.0) + bf_all[j, 0]
                bwd = (mm(bwd, m_all[i]) if n else 0.0) + bf_all[i, 1]

        xb_all[x] = zeros

        def from_rows(ref, rs, rows):
            for n in rows:

                @pl.when(x != n)
                def _():
                    remote(ref.at[n], ref.at[n], xb_ss.at[0], rs.at[n], partner).wait_recv()

        from_rows(xm_all, xm_rs, middle)
        both = mm(xm_all[2], xm_all[1])
        from_rows(xb_all, xb_rs, range(nx))
        v = [xb_all[n] for n in range(nx)]
        s_two = mm_nt(v[0], xm_all[1]) + v[1]
        s_three = mm_nt(v[0], both) + mm_nt(v[1], xm_all[2]) + v[2]
        s_row = jnp.where(x > 2, s_three, jnp.where(x > 1, s_two, jnp.where(x > 0, v[0], 0.0)))
        g_one = mm(v[3], xm_all[2]) + v[2]
        g_none = mm(v[3], both) + mm(v[2], xm_all[1]) + v[1]
        g_in = jnp.where(x < 1, g_none, jnp.where(x < 2, g_one, jnp.where(x < 3, v[3], 0.0)))
        for d in back + (0,):
            j = lax.rem(y + d, ny)
            sg_send[j, 0] = mm(s_row, pre[j, sl:]) + pre[j, :sl]
            sg_send[j, 1] = mm(g_in, suf[j, sl:]) + suf[j, :sl]
            if d:
                sg_copy(d).start()
        sg_all[slot] = sg_send[y]

    for n in range(HOLD):

        @pl.when(jnp.logical_or(slot != n, jnp.logical_not(holds)))
        def _():
            remote(sg_all.at[n], sg_all.at[n], a2_ss.at[0], a2_rs.at[n], partner).wait_recv()

    st = sg_all[:, 0].reshape(DK, DK)
    gt = sg_all[:, 1].reshape(DK, DK)

    u, w, dx_free, k_end, dx_state, ratio, ratio_t = (sv[n] for n in range(7))
    fresh = u - mm_nt(w, st)
    do = do_ref[...].astype(f32)
    d_qg = mm(do, st)
    dx = dx_free + mm_nt(dx_state, gt)
    d_ke = mm(fresh, gt)
    d_att = jnp.where(lower, mm_nt(do, fresh), 0.0)
    d_att_t = jnp.where(upper, mm_nt(fresh, do), 0.0)
    dy = -mm(dx, st)
    d_lo = jnp.where(row > col, -mm_nt(dx, fresh), 0.0)
    d_lo_t = jnp.where(row < col, -mm_nt(fresh, dx), 0.0)
    bare, lo, att, att_t, k, qn, y_in, lo_t = (sv[n] for n in range(7, 15))
    beta, grown, rest, k_scale, q_scale, sig = (cols[n] for n in range(6))
    q = qn * (DK ** (-0.5))
    v = proj_ref[2].astype(f32)
    sym = d_lo * ratio * beta + d_lo_t * ratio_t * beta_row
    dq = mm(d_att * ratio, k) + grown * d_qg
    dk = mm(d_att_t * ratio_t, q) + mm(sym, k) + (beta * grown) * dy + rest * d_ke
    ke_part = d_ke * k_end
    d_beta = row_sum(d_lo * bare + dx * v + grown * dy * k)
    mixed = d_lo * lo - d_lo_t * lo_t + d_att * att - d_att_t * att_t
    mixed = mixed + dy * y_in + d_qg * (grown * q) - ke_part
    dg_row = to_row(row_sum(mixed))
    tail = col_sum(row_sum(ke_part + last * (st * gt)))
    d_decay = row_sum(jnp.where(col >= row, dg_row, 0.0)) + tail
    d_l0 = -rate * sig * d_decay
    d_l1 = d_beta * beta * (1.0 - beta)
    dq = (q_scale * (DK ** (-0.5))) * (dq - qn * row_sum(dq * qn))
    dk = k_scale * (dk - k * row_sum(dk * k))
    dqk = jnp.concatenate([dq.astype(bf16), dk.astype(bf16)], 1)
    dv = (beta * dx).astype(bf16)

    loads[4].wait()
    loads[5].wait()
    wide_l0 = jnp.concatenate([d_l0, d_l0], 1)
    wide_l1 = jnp.concatenate([d_l1, d_l1], 1)

    def compute(d):
        at = pl.multiple_of(lax.rem(z + d + nz, nz) * (2 * DK), 2 * DK)
        here = pl.ds(at, 2 * DK)
        both = jnp.concatenate([wv[0, here, :], wv[1, here, :]], 1)
        out = dot(dqk, both, 1) + dot(dv, wv[2, here, :], 1)
        gates = gate_ref[:, here].astype(f32)
        out = out + wide_l0 * gates[0:1] + wide_l1 * gates[1:2]
        term[d % nz, 0] = out[:, :DK]
        term[d % nz, 1] = out[:, DK:]
        pair(d).start()

    def pair(d):
        d = d % nz
        return remote(term.at[d, 1 - c], pair_recv.at[d], p_ss.at[d], p_rs.at[d], partner)

    def summed(d):
        pair(d).wait_recv()
        return term[d % nz, c] + pair_recv[d % nz]

    part = DK // 2
    msgs = {
        ("far", 1): (0, pl.ds(0, part), 2),
        ("far", -1): (0, pl.ds(part, part), -2),
        ("mid", 1): (1, pl.ds(0, DK), 1),
        ("mid", -1): (2, pl.ds(0, DK), -1),
        ("two", 1): (3, pl.ds(0, DK), 2),
        ("two", -1): (4, pl.ds(0, DK), -2),
        ("one", 1): (5, pl.ds(0, DK), 1),
        ("one", -1): (6, pl.ds(0, DK), -1),
    }

    def msg(name):
        at, rows, d = msgs[name]
        n = list(msgs).index(name)
        return remote(
            z_send.at[at, rows], z_recv.at[at, rows], z_ss.at[n], z_rs.at[n], z_peer(d)
        )

    for d in (4, 3, -3):
        compute(d)
    compute(1)
    z_send[0] = summed(4)
    msg(("far", 1)).start()
    msg(("far", -1)).start()
    compute(-1)
    for sign in (1, -1):
        z_send[msgs["mid", sign][0]] = summed(3 * sign)
        msg(("mid", sign)).start()
    compute(2)
    compute(-2)
    compute(0)
    for sign in (1, -1):
        z_send[msgs["one", sign][0]] = summed(sign)
        msg(("one", sign)).start()
    two = {sign: summed(2 * sign) for sign in (1, -1)}
    total = summed(0)
    for sign in (1, -1):
        at = msgs["two", sign][0]
        msg(("far", sign)).wait_recv()
        msg(("mid", sign)).wait_recv()
        value = two[sign] + z_recv[msgs["mid", sign][0]]
        rows = msgs["far", sign][1]
        z_send[at] = value
        z_send[at, rows] = z_send[at, rows] + z_recv[0, rows]
        msg(("two", sign)).start()
    for sign in (1, -1):
        msg(("one", sign)).wait_recv()
        total = total + z_recv[msgs["one", sign][0]]
    for sign in (1, -1):
        msg(("two", sign)).wait_recv()
        total = total + z_recv[msgs["two", sign][0]]
    out_ref[...] = total.astype(bf16)

    to_holders(lambda n, dev: m_copy(n, dev).wait_send())
    to_holders(lambda n, dev: bf_copy(n, dev).wait_send())

    @pl.when(holds)
    def _():
        for d in range(1, nx):
            xb_copy(d).wait_send()

        @pl.when(in_middle)
        def _():
            for d in range(1, nx):
                xm_copy(d).wait_send()

        for d in range(1, ny):
            sg_copy(d).wait_send()

    for d in range(nz):
        pair(d).wait_send()
    for name in msgs:
        msg(name).wait_send()


def shards(nx, nz, projected, out_grad, logits, head_params, qkv_weight, gate_weight):
    head_params = head_params.T
    gate_weight = gate_weight.transpose(1, 0, 2).reshape(gate_weight.shape[0], -1)
    sl, ny = DK // HOLD, ROW
    dma = pltpu.SemaphoreType.DMA
    scratch = [
        pltpu.VMEM(projected.shape, bf16),
        pltpu.VMEM(out_grad.shape, bf16),
        pltpu.VMEM(logits.shape, f32),
        pltpu.VMEM(head_params.shape, f32),
        pltpu.VMEM(gate_weight.shape, bf16),
        pltpu.VMEM(qkv_weight.shape, bf16),
        pltpu.VMEM((15, DK, DK), f32),
        pltpu.VMEM((6, DK, DK), f32),
        pltpu.VMEM((ny, DK, DK), f32),
        pltpu.VMEM((HOLD, 2, sl, DK), f32),
        pltpu.VMEM((ny, 2, sl, DK), f32),
        pltpu.VMEM((ny, sl + DK, DK), f32),
        pltpu.VMEM((ny, sl + DK, DK), f32),
        pltpu.VMEM((nx, DK, DK), f32),
        pltpu.VMEM((2, sl, DK), f32),
        pltpu.VMEM((nx, sl, DK), f32),
        pltpu.VMEM((ny, 2, sl, DK), f32),
        pltpu.VMEM((HOLD, 2, sl, DK), f32),
        pltpu.VMEM((nz, 2, DK, DK), f32),
        pltpu.VMEM((nz, DK, DK), f32),
        pltpu.VMEM((7, DK, DK), f32),
        pltpu.VMEM((7, DK, DK), f32),
        dma((6,)),
        dma((HOLD,)),
        dma((ny,)),
        dma((HOLD,)),
        dma((ny,)),
        dma((nx - 1,)),
        dma((nx,)),
        dma((nx - 1,)),
        dma((nx,)),
        dma((ny,)),
        dma((HOLD,)),
        dma((nz,)),
        dma((nz,)),
        dma((12,)),
        dma((12,)),
    ]
    return pl.pallas_call(
        functools.partial(kernel, nx, nz),
        out_shape=pltpu.VMEM((DK, DK), bf16),
        in_specs=[pl.BlockSpec(memory_space=pltpu.HBM)] * 6,
        out_specs=pl.BlockSpec(memory_space=pltpu.VMEM),
        scratch_shapes=scratch,
        compiler_params=pltpu.CompilerParams(
            collective_id=0, has_side_effects=True, vmem_limit_bytes=48000000
        ),
        name="delta_backward",
    )(*(pltpu.with_memory_space_constraint(a, pltpu.HBM) for a in (projected, out_grad, logits, head_params, qkv_weight, gate_weight)))


def solution(mesh):
    nx, nz = mesh.shape["seq"] // ROW, mesh.shape["head"] // 2
    in_specs = (
        P(None, "seq", "head"),
        P("seq", "head"),
        P(None, "head", "seq"),
        P(None, "head"),
        P(None, None, "head"),
        P(None, "head", None),
    )
    return jax.shard_map(
        functools.partial(shards, nx, nz),
        mesh=mesh,
        in_specs=in_specs,
        out_specs=P("seq", "head"),
        check_vma=False,
    )
```
